32 devices in a mesh: outer: 4 (over y, core), inner: 8 (over z, x).
Axes of the slice: x: 2, y: 2, z: 4, core: 2. Of those that a mesh axis runs over, the one named last changes fastest.
Arguments:
- matrix_panel: float32 [32, 65536], P(None, ('outer', 'inner')), may hold values from -6 to 6
- row_signs: int32 [65536], P(('outer', 'inner')), may hold values from -1 to 1, as said below
- kept_rows: int32 [4096], replicated, may hold values from 0 to 65535, as said below
Outputs:
- sketch: float32 [4096, 32], P(('outer', 'inner'))
The draws below stay inside these ranges and needn't reach their ends.
Inputs may be any that keep to these rules, and one draw needn't show every extreme that they name: `row_signs`: each entry is -1 or 1. `kept_rows`: distinct row numbers.
All inputs are finite; a program needn't handle non-finite values.
Results may differ from the reference program's by a relative error of at most 0.00007.
Values sent between devices are 32-bit elements; how exact they have to be, the bound alone decides.
A program may use at most 64 MiB of HBM per device.

```python
import math
import jax
import jax.numpy as jnp
from jax import lax

COLS = 32
ROWS = 65536
KEPT = 4096


def draw_row_signs(key, part):
    return (2 * jax.random.randint(key, (ROWS,), 0, 2) - 1).astype(jnp.int32)


def draw_kept_rows(key, part):
    inside = jax.random.choice(jax.random.fold_in(key, 11), ROWS - 2, (KEPT - 2,), replace=False).astype(jnp.int32) + 1
    ends = jnp.array([0, ROWS - 1], dtype=jnp.int32)
    joined = jnp.concatenate([ends, inside])
    return jax.random.permutation(jax.random.fold_in(key, 23), joined).astype(jnp.int32)


def block_scale(rng, dims, split, low, top_value):
    loudness = 1.0
    for dim, shards_of in split:
        draws = jax.random.uniform(jax.random.fold_in(jax.random.fold_in(rng, 6), dim), (shards_of,), jnp.float32, low / len(split), top_value / len(split))
        loudness = loudness * jnp.repeat(jnp.exp(draws), dims[dim] // shards_of).reshape((-1,) + (1,) * (len(dims) - 1 - dim))
    return loudness


def noise(rng, dims, scale, bound, split=(), kind=jnp.bfloat16):
    loudness = block_scale(rng, dims, split, -0.22, 0.18) if split else 1.0
    result = jax.random.normal(rng, dims, jnp.float32) * scale * loudness
    return jnp.minimum(jnp.maximum(result, -bound), bound).astype(kind)


def setup_inputs(seed: int = 0) -> dict:
    key_of = jax.random.split(jax.random.key(seed), 4)
    return {
        "matrix_panel": noise(key_of[0], (COLS, ROWS), 1.0, 6.0, ((1, 32),), jnp.float32),
        "row_signs": draw_row_signs(jax.random.fold_in(key_of[3], 71), 0),
        "kept_rows": draw_kept_rows(jax.random.fold_in(key_of[3], 71), 0),
    }


def walsh_transform(vector):
    bit_total = ROWS.bit_length() - 1
    stride = 1
    done_bits = 0
    while done_bits < bit_total:
        if bit_total - done_bits >= 2:
            shaped = vector.reshape(-1, 4, stride)
            first = shaped[:, 0] + shaped[:, 1]
            second = shaped[:, 0] - shaped[:, 1]
            third = shaped[:, 2] + shaped[:, 3]
            fourth = shaped[:, 2] - shaped[:, 3]
            shaped = jnp.stack([first + third, second + fourth, first - third, second - fourth], axis=1)
            stride = stride * 4
            done_bits = done_bits + 2
        else:
            shaped = vector.reshape(-1, 2, stride)
            shaped = jnp.stack([shaped[:, 0] + shaped[:, 1], shaped[:, 0] - shaped[:, 1]], axis=1)
            stride = stride * 2
            done_bits = done_bits + 1
        vector = shaped.reshape(-1)
    return vector

def reference(matrix_panel, row_signs, kept_rows):
    signed = matrix_panel * row_signs.astype(jnp.float32)[None, :]

    def sketch_column(column):
        return walsh_transform(column)[kept_rows]
    picked = lax.map(sketch_column, signed)
    return picked.T * (1.0 / math.sqrt(ROWS))
```

```python
import functools
import math

import jax
import jax.numpy as jnp
from jax import lax
from jax.experimental import pallas as pl
from jax.experimental.pallas import tpu as pltpu
from jax.sharding import PartitionSpec as P

MESH = pl.DeviceIdType.MESH
LANES = 128
DEPTH = 256
PACK = 16


def bit_parity(values):
    folded = jnp.bitwise_xor(values, jnp.right_shift(values, 16))
    folded = jnp.bitwise_xor(folded, jnp.right_shift(folded, 8))
    folded = jnp.bitwise_xor(folded, jnp.right_shift(folded, 4))
    folded = jnp.bitwise_xor(folded, jnp.right_shift(folded, 2))
    folded = jnp.bitwise_xor(folded, jnp.right_shift(folded, 1))
    return jnp.bitwise_and(folded, 1)


def hadamard(order_size):
    positions = lax.iota(jnp.int32, order_size)
    shared = jnp.bitwise_and(positions[:, None], positions[None, :])
    return jnp.where(bit_parity(shared) == 0, 1.0, -1.0).astype(jnp.float32)


def scatter_form(matrix_panel, row_signs, kept_rows):
    highest = lax.Precision.HIGHEST
    columns, local_rows = matrix_panel.shape
    outer_count = lax.axis_size("outer")
    inner_count = lax.axis_size("inner")
    device_count = outer_count * inner_count
    total_rows = local_rows * device_count
    me_outer = lax.axis_index("outer")
    me_inner = lax.axis_index("inner")
    signed = matrix_panel * row_signs.astype(jnp.float32)[None, :]
    leading = 128
    trailing = local_rows // leading
    blocks = signed.reshape(columns, leading, trailing)
    blocks = jnp.einsum("ap,jpq->jaq", hadamard(leading), blocks, precision=highest)
    blocks = jnp.einsum("bq,jaq->jab", hadamard(trailing), blocks, precision=highest)
    local_mix = blocks.reshape(columns, local_rows)
    low_bits = kept_rows % local_rows
    high_outer = kept_rows // (local_rows * inner_count)
    high_inner = kept_rows // local_rows % inner_count
    flips = bit_parity(jnp.bitwise_and(high_outer, me_outer)) + bit_parity(
        jnp.bitwise_and(high_inner, me_inner)
    )
    parity_sign = jnp.where(flips % 2 == 0, 1.0, -1.0).astype(jnp.float32)
    values = jnp.take(local_mix, low_bits, axis=1)
    summed = lax.psum_scatter(
        (values * parity_sign[None, :]).T, ("outer", "inner"), scatter_dimension=0, tiled=True
    )
    return summed * (1.0 / math.sqrt(total_rows))


def log2(size):
    return size.bit_length() - 1


def sign_of_bit(rows, bit):
    return (1 - 2 * jnp.bitwise_and(jnp.right_shift(rows, bit), 1)).astype(jnp.float32)


def bit_of(index, bit):
    return index // (1 << bit) % 2


def flip_bits(index, mask):
    result, bit = index, 0
    while mask >> bit:
        if mask >> bit & 1:
            result = result + (1 - 2 * bit_of(index, bit)) * (1 << bit)
        bit += 1
    return result


def flip_all(index, mask, bits):
    result = 0
    for bit in range(bits):
        here, there = bit_of(index, bit), bit_of(mask, bit)
        result = result + (here + there - 2 * here * there) * (1 << bit)
    return result


def bit_weights(bits):
    guess = [44, 45, 35, 71, 47][:bits]
    signed = {0: 1}
    for weight in guess:
        grown = {}
        for total, count in signed.items():
            for sign in (-1, 0, 1):
                grown[total + sign * weight] = grown.get(total + sign * weight, 0) + count
        signed = grown
    if len(guess) == bits and signed[0] == 1:
        return guess
    return [1 << bit for bit in range(bits)]


def kernel(
    outer_count, inner_count, scale,
    panel_hbm, signs_hbm, kept_hbm, out_ref,
    panel_ref, signs_ref, kept_ref, upper_ref, lower_ref, mix_ref, bits_ref, send_ref, recv_ref,
    load_sem, swap_send, swap_recv, send_sem, recv_sem, ready_sem,
):
    device_count = outer_count * inner_count
    chip_count = device_count // 2
    chip_bits = log2(chip_count)
    inner_bits = log2(inner_count)
    columns, local_rows = panel_hbm.shape
    half = columns // 2
    mids = local_rows // DEPTH
    rows = 2 * mids * half
    me_outer = lax.axis_index("outer")
    me_inner = lax.axis_index("inner")
    me_core = me_outer % 2
    me_chip = me_outer // 2 * inner_count + me_inner
    partner = (me_outer + 1 - 2 * me_core, me_inner)

    def place_of(chip, core):
        return (chip // inner_count * 2 + core, chip % inner_count)

    own_rows = pl.ds(pl.multiple_of(me_core * half, half), half)
    other_rows = pl.ds(pl.multiple_of((1 - me_core) * half, half), half)
    loads = [
        pltpu.make_async_copy(source, target, load_sem.at[spot])
        for spot, (source, target) in enumerate(
            [
                (kept_hbm, kept_ref),
                (signs_hbm, signs_ref.at[me_core]),
                (panel_hbm.at[own_rows, :], panel_ref.at[me_core]),
            ]
        )
    ]
    for load in loads:
        load.start()

    weights = bit_weights(chip_bits + 1)
    late = [1 - me_core] + [bit_of(me_chip, bit) for bit in range(chip_bits)]
    steps = [weight * (1 - 2 * here) for weight, here in zip(weights, late)]
    ahead = [0]
    for step in steps:
        ahead = ahead + [total + step for total in ahead]

    def at(mask):
        return place_of(flip_bits(me_chip, mask >> 1), flip_bits(me_core, mask & 1))

    barrier = pltpu.get_barrier_semaphore()
    order = list(range(1, device_count))
    for mask in order:
        @pl.when(ahead[mask] > 0)
        def _(mask=mask):
            pl.semaphore_signal(barrier, inc=1, device_id=at(mask), device_id_type=MESH)

    earlier = 0
    for mask in order:
        earlier = earlier + jnp.where(ahead[mask] < 0, 1, 0)

    @pl.when(earlier > 0)
    def _():
        pl.semaphore_wait(barrier, earlier)

    for mask in order:
        @pl.when(ahead[mask] < 0)
        def _(mask=mask):
            pl.semaphore_signal(ready_sem.at[mask], inc=1, device_id=at(mask), device_id_type=MESH)

    @pl.when(ahead[1] > 0)
    def _():
        pl.semaphore_wait(ready_sem.at[1], 1)

    swaps = [
        pltpu.make_async_remote_copy(
            src_ref=source, dst_ref=target, send_sem=swap_send.at[spot], recv_sem=swap_recv.at[spot],
            device_id=partner, device_id_type=MESH,
        )
        for spot, (source, target) in enumerate(
            [(signs_hbm, signs_ref.at[me_core]), (panel_hbm.at[other_rows, :], panel_ref.at[me_core])]
        )
    ]
    for swap in swaps:
        swap.start()

    core_bit = log2(local_rows) + inner_bits
    chip_at = [log2(local_rows) + bit for bit in range(inner_bits)]
    chip_at += [core_bit + 1 + bit for bit in range(chip_bits - inner_bits)]
    fold_bits = [core_bit] + [bit for bit in reversed(range(log2(DEPTH), log2(local_rows)))]

    loads[0].wait()

    def signs_of(tile, carry):
        first = tile // inner_count * 2 * inner_count + tile % inner_count
        kept = jnp.concatenate(
            [
                kept_ref[:, pl.ds(pl.multiple_of(block * LANES, LANES), LANES)]
                for block in (first, first + inner_count)
            ],
            axis=1,
        )
        width = 2 * LANES
        for spot, bit in enumerate(fold_bits):
            bits_ref[tile, spot:spot + 1, :] = sign_of_bit(kept, bit)
        plane = jnp.full((1, width), scale, jnp.float32)
        for bit, position in enumerate(chip_at):
            plane = plane * jnp.where(bit_of(me_chip, bit) == 1, sign_of_bit(kept, position), 1.0)
        bits_ref[tile, len(fold_bits):len(fold_bits) + 1, :] = plane
        position = lax.broadcasted_iota(jnp.int32, (PACK, width), 0)
        base = jnp.ones((PACK, width), jnp.float32)
        for bit in range(log2(PACK)):
            taken = jnp.bitwise_and(jnp.right_shift(position, bit), 1) == 1
            base = base * jnp.where(taken, sign_of_bit(kept, bit), 1.0)
        blocks = [base.astype(jnp.bfloat16)]
        for bit in range(log2(PACK), log2(DEPTH)):
            flip = jnp.broadcast_to(sign_of_bit(kept, bit), (PACK, width)).astype(jnp.bfloat16)
            blocks = blocks + [block * flip for block in blocks]
        for top, block in enumerate(blocks):
            mix_ref[tile, top * PACK:(top + 1) * PACK, :] = block
        return carry

    lax.fori_loop(0, chip_count, signs_of, 0)

    def split(core):
        for mid in range(mids):
            lanes = slice(mid * DEPTH, (mid + 1) * DEPTH)
            block = panel_ref[core, :, lanes] * signs_ref[core, :, lanes].astype(jnp.float32)
            upper = block.astype(jnp.bfloat16)
            lower = (block - upper.astype(jnp.float32)).astype(jnp.bfloat16)
            upper_ref[core, mid * half:(mid + 1) * half, :] = upper
            lower_ref[core, mid * half:(mid + 1) * half, :] = lower

    for load in loads[1:]:
        load.wait()
    split(me_core)
    for swap in swaps:
        swap.wait_recv()
    split(1 - me_core)

    def part_of(tile):
        mix = mix_ref[tile]
        whole = jnp.dot(upper_ref[...].reshape(rows, DEPTH), mix, preferred_element_type=jnp.float32)
        whole = whole + jnp.dot(lower_ref[...].reshape(rows, DEPTH), mix, preferred_element_type=jnp.float32)
        for spot in range(len(fold_bits)):
            size = whole.shape[0] // 2
            whole = whole[:size] + whole[size:] * bits_ref[tile, spot:spot + 1, :]
        return whole * bits_ref[tile, len(fold_bits):len(fold_bits) + 1, :]

    my_rows = pl.ds(pl.multiple_of(me_core * half, half), half)

    def copy_to(chip, core, slot):
        return pltpu.make_async_remote_copy(
            src_ref=send_ref.at[slot],
            dst_ref=recv_ref.at[me_chip, my_rows, :],
            send_sem=send_sem.at[slot],
            recv_sem=recv_sem.at[me_chip * 2 + me_core],
            device_id=place_of(chip, core),
            device_id_type=MESH,
        )

    def dynamic_ahead(chip_mask, core_flip):
        total = steps[0] * core_flip
        for bit in range(chip_bits):
            total = total + steps[1 + bit] * bit_of(chip_mask, bit)
        return total

    last = chip_count - 1
    lead = jnp.where(me_chip == 0, last, me_chip)

    def send_tile(step, carry):
        plain = last - step
        mask = jnp.where(step == 0, lead, jnp.where(plain == lead, last, plain))
        chip = flip_all(me_chip, mask, chip_bits)
        part = part_of(chip)
        for core in range(2):
            slot = mask * 2 + core
            send_ref[slot] = part[:, core * LANES:(core + 1) * LANES]
            core_flip = jnp.where(me_core == core, 0, 1)

            @pl.when(dynamic_ahead(mask, core_flip) > 0)
            def _():
                pl.semaphore_wait(ready_sem.at[mask * 2 + core_flip], 1)

            copy_to(chip, core, slot).start()
        return carry

    lax.fori_loop(0, last, send_tile, 0)
    part = part_of(me_chip)
    for core in range(2):
        @pl.when(core == me_core)
        def _(core=core):
            recv_ref[me_chip, core * half:(core + 1) * half, :] = part[:, core * LANES:(core + 1) * LANES]

        @pl.when(core != me_core)
        def _(core=core):
            send_ref[core] = part[:, core * LANES:(core + 1) * LANES]
            copy_to(me_chip, core, core).start()

    def await_sent(slot, carry):
        copy_to(me_chip, 0, slot).wait_send()
        return carry

    def arrival(chip, core):
        return pltpu.make_async_remote_copy(
            src_ref=send_ref.at[0],
            dst_ref=recv_ref.at[chip, pl.ds(core * half, half), :],
            send_sem=send_sem.at[0],
            recv_sem=recv_sem.at[chip * 2 + core],
            device_id=partner,
            device_id_type=MESH,
        )

    for swap in swaps:
        swap.wait_send()
    lax.fori_loop(2, device_count, await_sent, 0)
    copy_to(me_chip, 0, 1 - me_core).wait_send()
    for core in range(2):
        @pl.when(core != me_core)
        def _(core=core):
            arrival(me_chip, core).wait_recv()

    def gather(mask, total):
        chip = flip_all(me_chip, mask, chip_bits)
        for core in range(2):
            arrival(chip, core).wait_recv()
        return total + recv_ref[chip]

    out_ref[...] = lax.fori_loop(1, chip_count, gather, recv_ref[me_chip])


def solution(mesh):
    outer_count, inner_count = mesh.shape["outer"], mesh.shape["inner"]
    device_count = outer_count * inner_count

    def local(matrix_panel, row_signs, kept_rows):
        columns, local_rows = matrix_panel.shape
        kept_count = kept_rows.shape[0]
        half = columns // 2
        powers = all(size & (size - 1) == 0 for size in (outer_count, inner_count, local_rows))
        fits = (
            powers
            and outer_count % 2 == 0
            and device_count >= 4
            and columns % (2 * PACK) == 0
            and kept_count == device_count * LANES
            and local_rows % (2 * DEPTH) == 0
        )
        if not fits:
            return scatter_form(matrix_panel, row_signs, kept_rows)
        mids = local_rows // DEPTH
        chips = device_count // 2
        arrived = pl.pallas_call(
            functools.partial(kernel, outer_count, inner_count, 1.0 / math.sqrt(local_rows * device_count)),
            out_shape=pltpu.VMEM((columns, LANES), jnp.float32),
            in_specs=[pl.BlockSpec(memory_space=pl.ANY)] * 3,
            out_specs=pl.BlockSpec(memory_space=pltpu.VMEM),
            scratch_shapes=[
                pltpu.VMEM((2, half, local_rows), jnp.float32),
                pltpu.VMEM((2, 1, local_rows), jnp.int32),
                pltpu.VMEM((1, kept_count), jnp.int32),
                pltpu.VMEM((2, mids * half, DEPTH), jnp.bfloat16),
                pltpu.VMEM((2, mids * half, DEPTH), jnp.bfloat16),
                pltpu.VMEM((chips, DEPTH, 2 * LANES), jnp.bfloat16),
                pltpu.VMEM((chips, 8, 2 * LANES), jnp.float32),
                pltpu.VMEM((device_count, half, LANES), jnp.float32),
                pltpu.VMEM((chips, columns, LANES), jnp.float32),
                pltpu.SemaphoreType.DMA((3,)),
                pltpu.SemaphoreType.DMA((2,)),
                pltpu.SemaphoreType.DMA((2,)),
                pltpu.SemaphoreType.DMA((device_count,)),
                pltpu.SemaphoreType.DMA((device_count,)),
                pltpu.SemaphoreType.REGULAR((device_count,)),
            ],
            compiler_params=pltpu.CompilerParams(collective_id=0, has_side_effects=True),
        )(matrix_panel, row_signs.reshape(1, local_rows), kept_rows.reshape(1, kept_count))
        return arrived.T

    return jax.shard_map(
        local,
        mesh=mesh,
        in_specs=(P(None, ("outer", "inner")), P(("outer", "inner")), P()),
        out_specs=P(("outer", "inner"), None),
        check_vma=False,
    )
```

```python
import functools
import math

import jax
import jax.numpy as jnp
from jax import lax
from jax.experimental import pallas as pl
from jax.experimental.pallas import tpu as pltpu
from jax.sharding import PartitionSpec as P

MESH = pl.DeviceIdType.MESH
LANES = 128
DEPTH = 256
PACK = 16


def bit_parity(values):
    folded = jnp.bitwise_xor(values, jnp.right_shift(values, 16))
    folded = jnp.bitwise_xor(folded, jnp.right_shift(folded, 8))
    folded = jnp.bitwise_xor(folded, jnp.right_shift(folded, 4))
    folded = jnp.bitwise_xor(folded, jnp.right_shift(folded, 2))
    folded = jnp.bitwise_xor(folded, jnp.right_shift(folded, 1))
    return jnp.bitwise_and(folded, 1)


def hadamard(order_size):
    positions = lax.iota(jnp.int32, order_size)
    shared = jnp.bitwise_and(positions[:, None], positions[None, :])
    return jnp.where(bit_parity(shared) == 0, 1.0, -1.0).astype(jnp.float32)


def scatter_form(matrix_panel, row_signs, kept_rows):
    highest = lax.Precision.HIGHEST
    columns, local_rows = matrix_panel.shape
    outer_count = lax.axis_size("outer")
    inner_count = lax.axis_size("inner")
    device_count = outer_count * inner_count
    total_rows = local_rows * device_count
    me_outer = lax.axis_index("outer")
    me_inner = lax.axis_index("inner")
    signed = matrix_panel * row_signs.astype(jnp.float32)[None, :]
    leading = 128
    trailing = local_rows // leading
    blocks = signed.reshape(columns, leading, trailing)
    blocks = jnp.einsum("ap,jpq->jaq", hadamard(leading), blocks, precision=highest)
    blocks = jnp.einsum("bq,jaq->jab", hadamard(trailing), blocks, precision=highest)
    local_mix = blocks.reshape(columns, local_rows)
    low_bits = kept_rows % local_rows
    high_outer = kept_rows // (local_rows * inner_count)
    high_inner = kept_rows // local_rows % inner_count
    flips = bit_parity(jnp.bitwise_and(high_outer, me_outer)) + bit_parity(
        jnp.bitwise_and(high_inner, me_inner)
    )
    parity_sign = jnp.where(flips % 2 == 0, 1.0, -1.0).astype(jnp.float32)
    values = jnp.take(local_mix, low_bits, axis=1)
    summed = lax.psum_scatter(
        (values * parity_sign[None, :]).T, ("outer", "inner"), scatter_dimension=0, tiled=True
    )
    return summed * (1.0 / math.sqrt(total_rows))


def log2(size):
    return size.bit_length() - 1


def sign_of_bit(rows, bit):
    return (1 - 2 * jnp.bitwise_and(jnp.right_shift(rows, bit), 1)).astype(jnp.float32)


def bit_of(index, bit):
    return jnp.bitwise_and(jnp.right_shift(index, bit), 1)


def kernel(
    outer_count, inner_count, scale,
    panel_hbm, signs_hbm, kept_hbm, out_ref,
    panel_ref, signs_ref, kept_ref, upper_ref, lower_ref, mix_ref, bits_ref, send_ref, recv_ref,
    load_sem, swap_send, swap_recv, send_sem, recv_sem, ready_sem,
):
    device_count = outer_count * inner_count
    chip_count = device_count // 2
    chip_bits = log2(chip_count)
    inner_bits = log2(inner_count)
    near_bits = min(1, inner_bits)
    far_bits = inner_bits - near_bits
    far_count = 1 << far_bits
    side_bits = chip_bits - far_bits
    side_count = 1 << side_bits
    columns, local_rows = panel_hbm.shape
    half = columns // 2
    mids = local_rows // DEPTH
    rows = 2 * mids * half
    me_outer = lax.axis_index("outer")
    me_inner = lax.axis_index("inner")
    me_core = bit_of(me_outer, 0)
    me_chip = jnp.right_shift(me_outer, 1) * inner_count + me_inner
    me_far = jnp.right_shift(me_inner, near_bits)
    me_side = jnp.right_shift(me_outer, 1) * (1 << near_bits) + jnp.bitwise_and(me_inner, (1 << near_bits) - 1)
    partner = (jnp.bitwise_xor(me_outer, 1), me_inner)

    own_rows = pl.ds(pl.multiple_of(me_core * half, half), half)
    other_rows = pl.ds(pl.multiple_of((1 - me_core) * half, half), half)
    loads = [
        pltpu.make_async_copy(source, target, load_sem.at[spot])
        for spot, (source, target) in enumerate(
            [
                (kept_hbm, kept_ref),
                (signs_hbm, signs_ref.at[me_core]),
                (panel_hbm.at[own_rows, :], panel_ref.at[me_core]),
            ]
        )
    ]

    groups = [[(0, 1)]]
    for bit in range(side_bits):
        groups.append([(mask, flip) for mask in range(1 << bit, 2 << bit) for flip in range(2)])
    for bit in range(far_bits):
        groups.append([
            (far * side_count + side, flip)
            for far in range(1 << bit, 2 << bit) for side in range(side_count) for flip in range(2)
        ])
    late = [1 - me_core] + [bit_of(me_side, bit) for bit in range(side_bits)]
    late += [bit_of(me_far, bit) for bit in range(far_bits)]
    outers = [jnp.bitwise_xor(me_outer, mask) for mask in range(outer_count)]
    inners = [jnp.bitwise_xor(me_inner, mask) for mask in range(inner_count)]

    def at(mask, flip):
        far, side = mask >> side_bits, mask & (side_count - 1)
        near = side & ((1 << near_bits) - 1)
        return (outers[(side >> near_bits) * 2 + flip], inners[(far << near_bits) + near])

    barrier = pltpu.get_barrier_semaphore()
    for group, here in reversed(list(zip(groups, late))):
        @pl.when(here == 0)
        def _(group=group):
            for mask, flip in group:
                pl.semaphore_signal(barrier, inc=1, device_id=at(mask, flip), device_id_type=MESH)

    for load in loads:
        load.start()
    earlier = (me_far * side_count + me_side) * 2 + 1 - me_core

    @pl.when(earlier > 0)
    def _():
        pl.semaphore_wait(barrier, earlier)

    swaps = [
        pltpu.make_async_remote_copy(
            src_ref=source, dst_ref=target, send_sem=swap_send.at[spot], recv_sem=swap_recv.at[spot],
            device_id=partner, device_id_type=MESH,
        )
        for spot, (source, target) in enumerate(
            [(signs_hbm, signs_ref.at[me_core]), (panel_hbm.at[other_rows, :], panel_ref.at[me_core])]
        )
    ]

    @pl.when(me_core == 0)
    def _():
        pl.semaphore_signal(ready_sem.at[far_count], inc=1, device_id=partner, device_id_type=MESH)
        for swap in swaps:
            swap.start()

    for group, here in reversed(list(zip(groups, late))[1:]):
        @pl.when(here == 1)
        def _(group=group):
            for mask, flip in group:
                pl.semaphore_signal(ready_sem.at[me_far], inc=1, device_id=at(mask, flip), device_id_type=MESH)

    @pl.when(me_core == 1)
    def _():
        pl.semaphore_wait(ready_sem.at[far_count], 1)
        for swap in swaps:
            swap.start()

    core_bit = log2(local_rows) + inner_bits
    chip_at = [log2(local_rows) + bit for bit in range(inner_bits)]
    chip_at += [core_bit + 1 + bit for bit in range(chip_bits - inner_bits)]
    fold_bits = [core_bit] + [bit for bit in reversed(range(log2(DEPTH), log2(local_rows)))]

    loads[0].wait()

    def signs_of(tile, carry):
        first = jnp.right_shift(tile, inner_bits) * 2 * inner_count + jnp.bitwise_and(tile, inner_count - 1)
        kept = jnp.concatenate(
            [
                kept_ref[:, pl.ds(pl.multiple_of(block * LANES, LANES), LANES)]
                for block in (first, first + inner_count)
            ],
            axis=1,
        )
        width = 2 * LANES
        for spot, bit in enumerate(fold_bits):
            bits_ref[tile, spot:spot + 1, :] = sign_of_bit(kept, bit)
        plane = jnp.full((1, width), scale, jnp.float32)
        for bit, position in enumerate(chip_at):
            plane = plane * jnp.where(bit_of(me_chip, bit) == 1, sign_of_bit(kept, position), 1.0)
        bits_ref[tile, len(fold_bits):len(fold_bits) + 1, :] = plane
        position = lax.broadcasted_iota(jnp.int32, (PACK, width), 0)
        base = jnp.ones((PACK, width), jnp.float32)
        for bit in range(log2(PACK)):
            taken = jnp.bitwise_and(jnp.right_shift(position, bit), 1) == 1
            base = base * jnp.where(taken, sign_of_bit(kept, bit), 1.0)
        blocks = [base.astype(jnp.bfloat16)]
        for bit in range(log2(PACK), log2(DEPTH)):
            flip = jnp.broadcast_to(sign_of_bit(kept, bit), (PACK, width)).astype(jnp.bfloat16)
            blocks = blocks + [block * flip for block in blocks]
        for top, block in enumerate(blocks):
            mix_ref[tile, top * PACK:(top + 1) * PACK, :] = block
        return carry

    lax.fori_loop(0, chip_count, signs_of, 0)

    def split(core):
        for mid in range(mids):
            lanes = slice(mid * DEPTH, (mid + 1) * DEPTH)
            block = panel_ref[core, :, lanes] * signs_ref[core, :, lanes].astype(jnp.float32)
            upper = block.astype(jnp.bfloat16)
            lower = (block - upper.astype(jnp.float32)).astype(jnp.bfloat16)
            upper_ref[core, mid * half:(mid + 1) * half, :] = upper
            lower_ref[core, mid * half:(mid + 1) * half, :] = lower

    for load in loads[1:]:
        load.wait()
    split(me_core)
    for swap in swaps:
        swap.wait_recv()
    split(1 - me_core)

    def part_of(tile):
        mix = mix_ref[tile]
        whole = jnp.dot(upper_ref[...].reshape(rows, DEPTH), mix, preferred_element_type=jnp.float32)
        whole = whole + jnp.dot(lower_ref[...].reshape(rows, DEPTH), mix, preferred_element_type=jnp.float32)
        for spot in range(len(fold_bits)):
            size = whole.shape[0] // 2
            whole = whole[:size] + whole[size:] * bits_ref[tile, spot:spot + 1, :]
        return whole * bits_ref[tile, len(fold_bits):len(fold_bits) + 1, :]

    last = chip_count - 1

    def mask_of(step):
        side = side_count - 1 - jnp.bitwise_and(step, side_count - 1)
        turn = jnp.right_shift(step, side_bits)
        far = far_count - 1 - turn
        if far_count == 4:
            far = jnp.where((me_far == 0) & (turn < 3), jnp.where(turn == 2, 3, 2 - turn), far)
        upper = jnp.right_shift(side, near_bits) * inner_count
        return upper + far * (1 << near_bits) + jnp.bitwise_and(side, (1 << near_bits) - 1)

    first = mask_of(0)
    at_zero = jnp.where(me_chip == 0, 1, 0)
    lead = me_chip * (1 - at_zero) + first * at_zero

    def send_tile(turn, carry):
        step = turn - 1
        plain = mask_of(jnp.maximum(step, 0))
        far = jnp.bitwise_xor(me_far, jnp.right_shift(jnp.bitwise_and(plain, inner_count - 1), near_bits))
        plain = jnp.where(plain == lead, first, plain)
        mask = jnp.where(turn == at_zero, lead, jnp.where(turn == 1 - at_zero, 0, plain))
        chip = jnp.bitwise_xor(me_chip, mask)
        inner = jnp.bitwise_and(chip, inner_count - 1)
        outer = jnp.right_shift(chip, inner_bits) * 2
        opens = (turn == 2 - at_zero) | ((turn > 2) & (jnp.bitwise_and(step, side_count - 1) == 0))
        wanted = jnp.where(far > me_far, 2 * side_count, jnp.where(far == me_far, 2 * (side_count - 1 - me_side), 0))

        @pl.when(opens & (wanted > 0))
        def _():
            pl.semaphore_wait(ready_sem.at[far], wanted)

        part = part_of(chip)
        for core in range(2):
            slot = turn * 2 + core
            piece = part[:, core * LANES:(core + 1) * LANES]
            own = (mask == 0) & (me_core == core)

            @pl.when(own)
            def _():
                recv_ref[me_chip * 2 + core] = piece

            @pl.when(jnp.logical_not(own))
            def _():
                send_ref[slot] = piece
                pltpu.make_async_remote_copy(
                    src_ref=send_ref.at[slot],
                    dst_ref=recv_ref.at[me_chip * 2 + me_core],
                    send_sem=send_sem,
                    recv_sem=recv_sem,
                    device_id=(outer + core, inner),
                    device_id_type=MESH,
                ).start()
        return carry

    lax.fori_loop(0, chip_count, send_tile, 0)
    for swap in swaps:
        swap.wait_send()
    everything = pltpu.make_async_remote_copy(
        src_ref=send_ref.at[pl.ds(0, device_count - 1)],
        dst_ref=recv_ref.at[pl.ds(0, device_count - 1)],
        send_sem=send_sem,
        recv_sem=recv_sem,
        device_id=partner,
        device_id_type=MESH,
    )
    everything.wait_send()
    everything.wait_recv()
    for core in range(2):
        terms = [recv_ref[chip * 2 + core] for chip in range(chip_count)]
        while len(terms) > 1:
            terms = [one + other for one, other in zip(terms[::2], terms[1::2])]
        out_ref[core * half:(core + 1) * half, :] = terms[0]


def solution(mesh):
    outer_count, inner_count = mesh.shape["outer"], mesh.shape["inner"]
    device_count = outer_count * inner_count

    def local(matrix_panel, row_signs, kept_rows):
        columns, local_rows = matrix_panel.shape
        kept_count = kept_rows.shape[0]
        half = columns // 2
        powers = all(size & (size - 1) == 0 for size in (outer_count, inner_count, local_rows))
        fits = (
            powers
            and outer_count % 2 == 0
            and device_count >= 4
            and columns % (2 * PACK) == 0
            and kept_count == device_count * LANES
            and local_rows % (2 * DEPTH) == 0
        )
        if not fits:
            return scatter_form(matrix_panel, row_signs, kept_rows)
        mids = local_rows // DEPTH
        chips = device_count // 2
        arrived = pl.pallas_call(
            functools.partial(kernel, outer_count, inner_count, 1.0 / math.sqrt(local_rows * device_count)),
            out_shape=pltpu.VMEM((columns, LANES), jnp.float32),
            in_specs=[pl.BlockSpec(memory_space=pl.ANY)] * 3,
            out_specs=pl.BlockSpec(memory_space=pltpu.VMEM),
            scratch_shapes=[
                pltpu.VMEM((2, half, local_rows), jnp.float32),
                pltpu.VMEM((2, 1, local_rows), jnp.int32),
                pltpu.VMEM((1, kept_count), jnp.int32),
                pltpu.VMEM((2, mids * half, DEPTH), jnp.bfloat16),
                pltpu.VMEM((2, mids * half, DEPTH), jnp.bfloat16),
                pltpu.VMEM((chips, DEPTH, 2 * LANES), jnp.bfloat16),
                pltpu.VMEM((chips, 8, 2 * LANES), jnp.float32),
                pltpu.VMEM((device_count, half, LANES), jnp.float32),
                pltpu.VMEM((device_count, half, LANES), jnp.float32),
                pltpu.SemaphoreType.DMA((3,)),
                pltpu.SemaphoreType.DMA((2,)),
                pltpu.SemaphoreType.DMA((2,)),
                pltpu.SemaphoreType.DMA(()),
                pltpu.SemaphoreType.DMA(()),
                pltpu.SemaphoreType.REGULAR((max(inner_count // 2, 1) + 1,)),
            ],
            compiler_params=pltpu.CompilerParams(collective_id=0, has_side_effects=True),
        )(matrix_panel, row_signs.reshape(1, local_rows), kept_rows.reshape(1, kept_count))
        return arrived.T

    return jax.shard_map(
        local,
        mesh=mesh,
        in_specs=(P(None, ("outer", "inner")), P(("outer", "inner")), P()),
        out_specs=P(("outer", "inner"), None),
        check_vma=False,
    )
```

```python
import functools
import math

import jax
import jax.numpy as jnp
from jax import lax
from jax.experimental import pallas as pl
from jax.experimental.pallas import tpu as pltpu
from jax.sharding import PartitionSpec as P

MESH = pl.DeviceIdType.MESH
LANES = 128
DEPTH = 256
PACK = 16
ROUTES = [[0, 1, 2, 3], [0, 2, 1, 3], [0, 1, 3, 2], [0, 1, 2, 3]]


def bit_parity(values):
    folded = jnp.bitwise_xor(values, jnp.right_shift(values, 16))
    folded = jnp.bitwise_xor(folded, jnp.right_shift(folded, 8))
    folded = jnp.bitwise_xor(folded, jnp.right_shift(folded, 4))
    folded = jnp.bitwise_xor(folded, jnp.right_shift(folded, 2))
    folded = jnp.bitwise_xor(folded, jnp.right_shift(folded, 1))
    return jnp.bitwise_and(folded, 1)


def hadamard(order_size):
    positions = lax.iota(jnp.int32, order_size)
    shared = jnp.bitwise_and(positions[:, None], positions[None, :])
    return jnp.where(bit_parity(shared) == 0, 1.0, -1.0).astype(jnp.float32)


def scatter_form(matrix_panel, row_signs, kept_rows):
    highest = lax.Precision.HIGHEST
    columns, local_rows = matrix_panel.shape
    outer_count = lax.axis_size("outer")
    inner_count = lax.axis_size("inner")
    device_count = outer_count * inner_count
    total_rows = local_rows * device_count
    me_outer = lax.axis_index("outer")
    me_inner = lax.axis_index("inner")
    signed = matrix_panel * row_signs.astype(jnp.float32)[None, :]
    leading = 128
    trailing = local_rows // leading
    blocks = signed.reshape(columns, leading, trailing)
    blocks = jnp.einsum("ap,jpq->jaq", hadamard(leading), blocks, precision=highest)
    blocks = jnp.einsum("bq,jaq->jab", hadamard(trailing), blocks, precision=highest)
    local_mix = blocks.reshape(columns, local_rows)
    low_bits = kept_rows % local_rows
    high_outer = kept_rows // (local_rows * inner_count)
    high_inner = kept_rows // local_rows % inner_count
    flips = bit_parity(jnp.bitwise_and(high_outer, me_outer)) + bit_parity(
        jnp.bitwise_and(high_inner, me_inner)
    )
    parity_sign = jnp.where(flips % 2 == 0, 1.0, -1.0).astype(jnp.float32)
    values = jnp.take(local_mix, low_bits, axis=1)
    summed = lax.psum_scatter(
        (values * parity_sign[None, :]).T, ("outer", "inner"), scatter_dimension=0, tiled=True
    )
    return summed * (1.0 / math.sqrt(total_rows))


def log2(size):
    return size.bit_length() - 1


def sign_of_bit(rows, bit):
    return (1 - 2 * jnp.bitwise_and(jnp.right_shift(rows, bit), 1)).astype(jnp.float32)


def bit_of(index, bit):
    return jnp.bitwise_and(jnp.right_shift(index, bit), 1)


def kernel(
    outer_count, inner_count, scale,
    panel_hbm, signs_hbm, kept_hbm, out_ref,
    panel_ref, signs_ref, kept_ref, upper_ref, lower_ref, mix_ref, bits_ref, send_ref, recv_ref,
    load_sem, swap_send, swap_recv, send_sem, recv_sem, ready_sem,
):
    device_count = outer_count * inner_count
    chip_count = device_count // 2
    chip_bits = log2(chip_count)
    inner_bits = log2(inner_count)
    near_bits = min(1, inner_bits)
    far_bits = inner_bits - near_bits
    far_count = 1 << far_bits
    side_bits = chip_bits - far_bits
    side_count = 1 << side_bits
    columns, local_rows = panel_hbm.shape
    half = columns // 2
    mids = local_rows // DEPTH
    rows = 2 * mids * half
    me_outer = lax.axis_index("outer")
    me_inner = lax.axis_index("inner")
    me_core = bit_of(me_outer, 0)
    me_chip = jnp.right_shift(me_outer, 1) * inner_count + me_inner
    me_far = jnp.right_shift(me_inner, near_bits)
    me_side = jnp.right_shift(me_outer, 1) * (1 << near_bits) + jnp.bitwise_and(me_inner, (1 << near_bits) - 1)
    partner = (jnp.bitwise_xor(me_outer, 1), me_inner)

    own_rows = pl.ds(pl.multiple_of(me_core * half, half), half)
    other_rows = pl.ds(pl.multiple_of((1 - me_core) * half, half), half)
    loads = [
        pltpu.make_async_copy(source, target, load_sem.at[spot])
        for spot, (source, target) in enumerate(
            [
                (kept_hbm, kept_ref),
                (signs_hbm, signs_ref.at[me_core]),
                (panel_hbm.at[own_rows, :], panel_ref.at[me_core]),
            ]
        )
    ]

    for load in loads:
        load.start()

    groups = [[(0, 1)]]
    for bit in range(side_bits):
        groups.append([(mask, flip) for mask in range(1 << bit, 2 << bit) for flip in range(2)])
    for bit in range(far_bits):
        groups.append([
            (far * side_count + side, flip)
            for far in range(1 << bit, 2 << bit) for side in range(side_count) for flip in range(2)
        ])
    late = [1 - me_core] + [bit_of(me_side, bit) for bit in range(side_bits)]
    late += [bit_of(me_far, bit) for bit in range(far_bits)]
    outers = [jnp.bitwise_xor(me_outer, mask) for mask in range(outer_count)]
    inners = [jnp.bitwise_xor(me_inner, mask) for mask in range(inner_count)]

    def at(mask, flip):
        far, side = mask >> side_bits, mask & (side_count - 1)
        near = side & ((1 << near_bits) - 1)
        return (outers[(side >> near_bits) * 2 + flip], inners[(far << near_bits) + near])

    barrier = pltpu.get_barrier_semaphore()
    for group, here in reversed(list(zip(groups, late))):
        @pl.when(here == 0)
        def _(group=group):
            for mask, flip in group:
                pl.semaphore_signal(barrier, inc=1, device_id=at(mask, flip), device_id_type=MESH)

    earlier = (me_far * side_count + me_side) * 2 + 1 - me_core

    @pl.when(earlier > 0)
    def _():
        pl.semaphore_wait(barrier, earlier)

    swaps = [
        pltpu.make_async_remote_copy(
            src_ref=source, dst_ref=target, send_sem=swap_send.at[spot], recv_sem=swap_recv.at[spot],
            device_id=partner, device_id_type=MESH,
        )
        for spot, (source, target) in enumerate(
            [(signs_hbm, signs_ref.at[me_core]), (panel_hbm.at[other_rows, :], panel_ref.at[me_core])]
        )
    ]

    @pl.when(me_core == 0)
    def _():
        pl.semaphore_signal(ready_sem.at[far_count], inc=1, device_id=partner, device_id_type=MESH)
        for swap in swaps:
            swap.start()

    for group, here in reversed(list(zip(groups, late))[1:]):
        @pl.when(here == 1)
        def _(group=group):
            for mask, flip in group:
                pl.semaphore_signal(ready_sem.at[me_far], inc=1, device_id=at(mask, flip), device_id_type=MESH)

    @pl.when(me_core == 1)
    def _():
        pl.semaphore_wait(ready_sem.at[far_count], 1)
        for swap in swaps:
            swap.start()

    core_bit = log2(local_rows) + inner_bits
    chip_at = [log2(local_rows) + bit for bit in range(inner_bits)]
    chip_at += [core_bit + 1 + bit for bit in range(chip_bits - inner_bits)]
    fold_bits = [core_bit] + [bit for bit in reversed(range(log2(DEPTH), log2(local_rows)))]

    loads[0].wait()

    def signs_of(tile, carry):
        first = jnp.right_shift(tile, inner_bits) * 2 * inner_count + jnp.bitwise_and(tile, inner_count - 1)
        kept = jnp.concatenate(
            [
                kept_ref[:, pl.ds(pl.multiple_of(block * LANES, LANES), LANES)]
                for block in (first, first + inner_count)
            ],
            axis=1,
        )
        width = 2 * LANES
        for spot, bit in enumerate(fold_bits):
            bits_ref[tile, spot:spot + 1, :] = sign_of_bit(kept, bit)
        plane = jnp.full((1, width), scale, jnp.float32)
        for bit, position in enumerate(chip_at):
            plane = plane * jnp.where(bit_of(me_chip, bit) == 1, sign_of_bit(kept, position), 1.0)
        bits_ref[tile, len(fold_bits):len(fold_bits) + 1, :] = plane
        position = lax.broadcasted_iota(jnp.int32, (PACK, width), 0)
        base = jnp.ones((PACK, width), jnp.float32)
        for bit in range(log2(PACK)):
            taken = jnp.bitwise_and(jnp.right_shift(position, bit), 1) == 1
            base = base * jnp.where(taken, sign_of_bit(kept, bit), 1.0)
        blocks = [base.astype(jnp.bfloat16)]
        for bit in range(log2(PACK), log2(DEPTH)):
            flip = jnp.broadcast_to(sign_of_bit(kept, bit), (PACK, width)).astype(jnp.bfloat16)
            blocks = blocks + [block * flip for block in blocks]
        for top, block in enumerate(blocks):
            mix_ref[tile, top * PACK:(top + 1) * PACK, :] = block
        return carry

    lax.fori_loop(0, chip_count, signs_of, 0)

    def split(core):
        for mid in range(mids):
            lanes = slice(mid * DEPTH, (mid + 1) * DEPTH)
            block = panel_ref[core, :, lanes] * signs_ref[core, :, lanes].astype(jnp.float32)
            upper = block.astype(jnp.bfloat16)
            lower = (block - upper.astype(jnp.float32)).astype(jnp.bfloat16)
            upper_ref[core, mid * half:(mid + 1) * half, :] = upper
            lower_ref[core, mid * half:(mid + 1) * half, :] = lower

    for load in loads[1:]:
        load.wait()
    split(me_core)
    for swap in swaps:
        swap.wait_recv()
    split(1 - me_core)

    def parts_of(tiles):
        upper = upper_ref[...].reshape(rows, DEPTH)
        lower = lower_ref[...].reshape(rows, DEPTH)
        parts = []
        for tile in tiles:
            mix = mix_ref[tile]
            part = jnp.dot(upper, mix, preferred_element_type=jnp.float32)
            parts.append(part + jnp.dot(lower, mix, preferred_element_type=jnp.float32))
        for spot in range(len(fold_bits)):
            size = rows >> (spot + 1)
            parts = [
                part[:size] + part[size:] * bits_ref[tile, spot:spot + 1, :] for part, tile in zip(parts, tiles)
            ]
        plane = len(fold_bits)
        return [part * bits_ref[tile, plane:plane + 1, :] for part, tile in zip(parts, tiles)]

    route = 0
    for here, planes in enumerate(ROUTES):
        route = jnp.where(me_far == here, sum((plane ^ here) << 2 * turn for turn, plane in enumerate(planes)), route)

    def mask_of(step):
        side = side_count - 1 - jnp.bitwise_and(step, side_count - 1)
        turn = jnp.right_shift(step, side_bits)
        far = far_count - 1 - turn
        if far_count == 4:
            far = jnp.bitwise_and(jnp.right_shift(route, 2 * turn), 3)
        upper = jnp.right_shift(side, near_bits) * inner_count
        return upper + far * (1 << near_bits) + jnp.bitwise_and(side, (1 << near_bits) - 1)

    mine = me_chip * 2 + me_core
    at_zero = jnp.where(me_chip == 0, 1, 0)

    def own_at(slot):
        @pl.when(me_core == 0)
        def _():
            recv_ref[mine] = send_ref[slot]

        @pl.when(me_core == 1)
        def _():
            recv_ref[mine] = send_ref[slot + 1]

    def start(slot, chip, core):
        pltpu.make_async_remote_copy(
            src_ref=send_ref.at[slot + core],
            dst_ref=recv_ref.at[mine],
            send_sem=send_sem,
            recv_sem=recv_sem,
            device_id=(jnp.right_shift(chip, inner_bits) * 2 + core, jnp.bitwise_and(chip, inner_count - 1)),
            device_id_type=MESH,
        ).start()

    def start_both(slot, chip):
        own = chip == me_chip
        for core in range(2):
            @pl.when(jnp.logical_not(own & (me_core == core)))
            def _(core=core):
                start(slot, chip, core)

        @pl.when(own)
        def _():
            own_at(slot)

    def keep(slot, part):
        send_ref[slot] = part[:, :LANES]
        send_ref[slot + 1] = part[:, LANES:]

    keep(device_count, parts_of([0])[0])
    start_both(device_count, 0)

    def send_turn(turn, carry):
        masks = [mask_of(turn * side_count + side) for side in range(side_count)]
        far = jnp.bitwise_xor(me_far, jnp.right_shift(jnp.bitwise_and(masks[0], inner_count - 1), near_bits))
        skip = masks[-1] == 0
        masks = [jnp.where(mask == me_chip, mask_of(0), mask) for mask in masks]
        masks[0] = jnp.where(turn == 0, mask_of(0) * at_zero, masks[0])
        chips = [jnp.bitwise_xor(me_chip, mask) for mask in masks]
        for side, part in enumerate(parts_of(chips)):
            keep((turn * side_count + side) * 2, part)
        wanted = jnp.where(far > me_far, 2 * side_count, jnp.where(far == me_far, 2 * (side_count - 1 - me_side), 0))

        @pl.when(wanted > 0)
        def _():
            pl.semaphore_wait(ready_sem.at[far], wanted)

        for side, chip in enumerate(chips):
            slot = (turn * side_count + side) * 2
            if side == 0:
                start_both(slot, chip)
            elif side == side_count - 1:
                @pl.when(jnp.logical_not(skip))
                def _():
                    start(slot, chip, 0)
                    start(slot, chip, 1)
            else:
                start(slot, chip, 0)
                start(slot, chip, 1)
        return carry

    lax.fori_loop(0, far_count, send_turn, 0)
    for swap in swaps:
        swap.wait_send()
    everything = pltpu.make_async_remote_copy(
        src_ref=send_ref.at[pl.ds(0, device_count - 1)],
        dst_ref=recv_ref.at[pl.ds(0, device_count - 1)],
        send_sem=send_sem,
        recv_sem=recv_sem,
        device_id=partner,
        device_id_type=MESH,
    )
    everything.wait_send()
    everything.wait_recv()
    for core in range(2):
        terms = [recv_ref[chip * 2 + core] for chip in range(chip_count)]
        while len(terms) > 1:
            terms = [one + other for one, other in zip(terms[::2], terms[1::2])]
        out_ref[core * half:(core + 1) * half, :] = terms[0]


def solution(mesh):
    outer_count, inner_count = mesh.shape["outer"], mesh.shape["inner"]
    device_count = outer_count * inner_count

    def local(matrix_panel, row_signs, kept_rows):
        columns, local_rows = matrix_panel.shape
        kept_count = kept_rows.shape[0]
        half = columns // 2
        powers = all(size & (size - 1) == 0 for size in (outer_count, inner_count, local_rows))
        fits = (
            powers
            and outer_count % 2 == 0
            and device_count >= 4
            and columns % (2 * PACK) == 0
            and kept_count == device_count * LANES
            and local_rows % (2 * DEPTH) == 0
        )
        if not fits:
            return scatter_form(matrix_panel, row_signs, kept_rows)
        mids = local_rows // DEPTH
        chips = device_count // 2
        arrived = pl.pallas_call(
            functools.partial(kernel, outer_count, inner_count, 1.0 / math.sqrt(local_rows * device_count)),
            out_shape=pltpu.VMEM((columns, LANES), jnp.float32),
            in_specs=[pl.BlockSpec(memory_space=pl.ANY)] * 3,
            out_specs=pl.BlockSpec(memory_space=pltpu.VMEM),
            scratch_shapes=[
                pltpu.VMEM((2, half, local_rows), jnp.float32),
                pltpu.VMEM((2, 1, local_rows), jnp.int32),
                pltpu.VMEM((1, kept_count), jnp.int32),
                pltpu.VMEM((2, mids * half, DEPTH), jnp.bfloat16),
                pltpu.VMEM((2, mids * half, DEPTH), jnp.bfloat16),
                pltpu.VMEM((chips, DEPTH, 2 * LANES), jnp.bfloat16),
                pltpu.VMEM((chips, 8, 2 * LANES), jnp.float32),
                pltpu.VMEM((device_count + 2, half, LANES), jnp.float32),
                pltpu.VMEM((device_count, half, LANES), jnp.float32),
                pltpu.SemaphoreType.DMA((3,)),
                pltpu.SemaphoreType.DMA((2,)),
                pltpu.SemaphoreType.DMA((2,)),
                pltpu.SemaphoreType.DMA(()),
                pltpu.SemaphoreType.DMA(()),
                pltpu.SemaphoreType.REGULAR((max(inner_count // 2, 1) + 1,)),
            ],
            compiler_params=pltpu.CompilerParams(collective_id=0, has_side_effects=True),
        )(matrix_panel, row_signs.reshape(1, local_rows), kept_rows.reshape(1, kept_count))
        return arrived.T

    return jax.shard_map(
        local,
        mesh=mesh,
        in_specs=(P(None, ("outer", "inner")), P(("outer", "inner")), P()),
        out_specs=P(("outer", "inner"), None),
        check_vma=False,
    )
```

```python
import functools
import math

import jax
import jax.numpy as jnp
from jax import lax
from jax.experimental import pallas as pl
from jax.experimental.pallas import tpu as pltpu
from jax.sharding import PartitionSpec as P

MESH = pl.DeviceIdType.MESH
LANES = 128
DEPTH = 256
PACK = 16
GROUPS = [4, 4, 4, 4]
LEADS = [1, 1, 1, 1]
ROUTES = [[(0, 3), (0, 2), (0, 1), (0, 0), (1, 3), (1, 2), (1, 1), (1, 0), (2, 3), (2, 2), (2, 1), (2, 0), (3, 3), (3, 2), (3, 1), (3, 0)], [(0, 3), (0, 2), (0, 1), (0, 0), (2, 3), (2, 2), (2, 1), (2, 0), (1, 3), (1, 2), (1, 1), (1, 0), (3, 3), (3, 2), (3, 1), (3, 0)], [(0, 3), (0, 2), (0, 1), (0, 0), (1, 3), (1, 2), (1, 1), (1, 0), (3, 3), (3, 2), (3, 1), (3, 0), (2, 3), (2, 2), (2, 1), (2, 0)], [(0, 3), (0, 2), (0, 1), (0, 0), (1, 3), (1, 2), (1, 1), (1, 0), (2, 3), (2, 2), (2, 1), (2, 0), (3, 3), (3, 2), (3, 1), (3, 0)]]


def bit_parity(values):
    folded = jnp.bitwise_xor(values, jnp.right_shift(values, 16))
    folded = jnp.bitwise_xor(folded, jnp.right_shift(folded, 8))
    folded = jnp.bitwise_xor(folded, jnp.right_shift(folded, 4))
    folded = jnp.bitwise_xor(folded, jnp.right_shift(folded, 2))
    folded = jnp.bitwise_xor(folded, jnp.right_shift(folded, 1))
    return jnp.bitwise_and(folded, 1)


def hadamard(order_size):
    positions = lax.iota(jnp.int32, order_size)
    shared = jnp.bitwise_and(positions[:, None], positions[None, :])
    return jnp.where(bit_parity(shared) == 0, 1.0, -1.0).astype(jnp.float32)


def scatter_form(matrix_panel, row_signs, kept_rows):
    highest = lax.Precision.HIGHEST
    columns, local_rows = matrix_panel.shape
    outer_count = lax.axis_size("outer")
    inner_count = lax.axis_size("inner")
    device_count = outer_count * inner_count
    total_rows = local_rows * device_count
    me_outer = lax.axis_index("outer")
    me_inner = lax.axis_index("inner")
    signed = matrix_panel * row_signs.astype(jnp.float32)[None, :]
    leading = 128
    trailing = local_rows // leading
    blocks = signed.reshape(columns, leading, trailing)
    blocks = jnp.einsum("ap,jpq->jaq", hadamard(leading), blocks, precision=highest)
    blocks = jnp.einsum("bq,jaq->jab", hadamard(trailing), blocks, precision=highest)
    local_mix = blocks.reshape(columns, local_rows)
    low_bits = kept_rows % local_rows
    high_outer = kept_rows // (local_rows * inner_count)
    high_inner = kept_rows // local_rows % inner_count
    flips = bit_parity(jnp.bitwise_and(high_outer, me_outer)) + bit_parity(
        jnp.bitwise_and(high_inner, me_inner)
    )
    parity_sign = jnp.where(flips % 2 == 0, 1.0, -1.0).astype(jnp.float32)
    values = jnp.take(local_mix, low_bits, axis=1)
    summed = lax.psum_scatter(
        (values * parity_sign[None, :]).T, ("outer", "inner"), scatter_dimension=0, tiled=True
    )
    return summed * (1.0 / math.sqrt(total_rows))


def log2(size):
    return size.bit_length() - 1


def sign_of_bit(rows, bit):
    return (1 - 2 * jnp.bitwise_and(jnp.right_shift(rows, bit), 1)).astype(jnp.float32)


def bit_of(index, bit):
    return jnp.bitwise_and(jnp.right_shift(index, bit), 1)


def routes(far_count, side_count):
    if far_count == len(ROUTES) and side_count == 4:
        return ROUTES
    return [[(far, side) for far in range(far_count) for side in reversed(range(side_count))] for _ in range(far_count)]


def kernel(
    outer_count, inner_count, scale,
    panel_hbm, signs_hbm, kept_hbm, out_ref,
    panel_ref, signs_ref, kept_ref, upper_ref, lower_ref, mix_ref, bits_ref, send_ref, recv_ref,
    load_sem, swap_send, swap_recv, send_sem, recv_sem, ready_sem,
):
    device_count = outer_count * inner_count
    chip_count = device_count // 2
    chip_bits = log2(chip_count)
    inner_bits = log2(inner_count)
    near_bits = min(1, inner_bits)
    far_bits = inner_bits - near_bits
    far_count = 1 << far_bits
    side_bits = chip_bits - far_bits
    side_count = 1 << side_bits
    columns, local_rows = panel_hbm.shape
    half = columns // 2
    mids = local_rows // DEPTH
    rows = 2 * mids * half
    me_outer = lax.axis_index("outer")
    me_inner = lax.axis_index("inner")
    me_core = bit_of(me_outer, 0)
    me_chip = jnp.right_shift(me_outer, 1) * inner_count + me_inner
    me_far = jnp.right_shift(me_inner, near_bits)
    me_side = jnp.right_shift(me_outer, 1) * (1 << near_bits) + jnp.bitwise_and(me_inner, (1 << near_bits) - 1)
    partner = (jnp.bitwise_xor(me_outer, 1), me_inner)

    own_rows = pl.ds(pl.multiple_of(me_core * half, half), half)
    other_rows = pl.ds(pl.multiple_of((1 - me_core) * half, half), half)
    loads = [
        pltpu.make_async_copy(source, target, load_sem.at[spot])
        for spot, (source, target) in enumerate(
            [
                (kept_hbm, kept_ref),
                (signs_hbm, signs_ref.at[me_core]),
                (panel_hbm.at[own_rows, :], panel_ref.at[me_core]),
            ]
        )
    ]

    for load in loads:
        load.start()

    groups = [[1 << bit | rest for rest in range(1 << bit)] for bit in range(chip_bits)]
    late = [bit_of(me_side, bit) for bit in range(side_bits)] + [bit_of(me_far, bit) for bit in range(far_bits)]
    outers = [jnp.bitwise_xor(me_outer - me_core, mask) for mask in range(0, outer_count, 2)]
    inners = [jnp.bitwise_xor(me_inner, mask) for mask in range(inner_count)]
    pair, relay = far_count, far_count + 1

    def at(mask, core):
        far, side = mask >> side_bits, mask & (side_count - 1)
        near = side & ((1 << near_bits) - 1)
        return (outers[side >> near_bits] + core, inners[(far << near_bits) + near])

    def tell(semaphore, device):
        pl.semaphore_signal(semaphore, inc=1, device_id=device, device_id_type=MESH)

    barrier = pltpu.get_barrier_semaphore()

    @pl.when(me_core == 0)
    def _():
        tell(barrier, partner)

    for group, here in reversed(list(zip(groups, late))):
        @pl.when(here == 0)
        def _(group=group):
            for mask in group:
                tell(barrier, at(mask, 0))

    swaps = [
        pltpu.make_async_remote_copy(
            src_ref=source, dst_ref=target, send_sem=swap_send.at[spot], recv_sem=swap_recv.at[spot],
            device_id=partner, device_id_type=MESH,
        )
        for spot, (source, target) in enumerate(
            [(signs_hbm, signs_ref.at[me_core]), (panel_hbm.at[other_rows, :], panel_ref.at[me_core])]
        )
    ]

    @pl.when(me_core == 1)
    def _():
        pl.semaphore_wait(barrier, 1)
        tell(ready_sem.at[pair], partner)

    @pl.when(me_core == 0)
    def _():
        pl.semaphore_wait(ready_sem.at[pair], 1)

    for swap in swaps:
        swap.start()

    earlier = me_far * side_count + me_side

    def settle():
        @pl.when(earlier > 0)
        def _():
            pl.semaphore_wait(barrier, 2 * earlier)

        tell(ready_sem.at[relay], partner)
        for group, here in reversed(list(zip(groups, late))):
            @pl.when(here == 1)
            def _(group=group):
                for mask in group:
                    for core in range(2):
                        tell(ready_sem.at[me_far], at(mask, core))

    @pl.when((me_core == 0) & (earlier == chip_count - 1))
    def _():
        settle()

    core_bit = log2(local_rows) + inner_bits
    chip_at = [log2(local_rows) + bit for bit in range(inner_bits)]
    chip_at += [core_bit + 1 + bit for bit in range(chip_bits - inner_bits)]
    fold_bits = [core_bit] + [bit for bit in reversed(range(log2(DEPTH), log2(local_rows)))]

    loads[0].wait()

    def signs_of(tile, carry):
        first = jnp.right_shift(tile, inner_bits) * 2 * inner_count + jnp.bitwise_and(tile, inner_count - 1)
        kept = jnp.concatenate(
            [
                kept_ref[:, pl.ds(pl.multiple_of(block * LANES, LANES), LANES)]
                for block in (first, first + inner_count)
            ],
            axis=1,
        )
        width = 2 * LANES
        for spot, bit in enumerate(fold_bits):
            bits_ref[tile, spot:spot + 1, :] = sign_of_bit(kept, bit)
        plane = jnp.full((1, width), scale, jnp.float32)
        for bit, position in enumerate(chip_at):
            plane = plane * jnp.where(bit_of(me_chip, bit) == 1, sign_of_bit(kept, position), 1.0)
        bits_ref[tile, len(fold_bits):len(fold_bits) + 1, :] = plane
        position = lax.broadcasted_iota(jnp.int32, (PACK, width), 0)
        base = jnp.ones((PACK, width), jnp.float32)
        for bit in range(log2(PACK)):
            taken = jnp.bitwise_and(jnp.right_shift(position, bit), 1) == 1
            base = base * jnp.where(taken, sign_of_bit(kept, bit), 1.0)
        blocks = [base.astype(jnp.bfloat16)]
        for bit in range(log2(PACK), log2(DEPTH)):
            flip = jnp.broadcast_to(sign_of_bit(kept, bit), (PACK, width)).astype(jnp.bfloat16)
            blocks = blocks + [block * flip for block in blocks]
        for top, block in enumerate(blocks):
            mix_ref[tile, top * PACK:(top + 1) * PACK, :] = block
        return carry

    lax.fori_loop(0, chip_count, signs_of, 0)

    @pl.when((me_core == 0) & (earlier < chip_count - 1))
    def _():
        settle()


    def split(core):
        for mid in range(mids):
            lanes = slice(mid * DEPTH, (mid + 1) * DEPTH)
            block = panel_ref[core, :, lanes] * signs_ref[core, :, lanes].astype(jnp.float32)
            upper = block.astype(jnp.bfloat16)
            lower = (block - upper.astype(jnp.float32)).astype(jnp.bfloat16)
            upper_ref[core, mid * half:(mid + 1) * half, :] = upper
            lower_ref[core, mid * half:(mid + 1) * half, :] = lower

    for load in loads[1:]:
        load.wait()
    split(me_core)
    for swap in swaps:
        swap.wait_recv()
    split(1 - me_core)

    def parts_of(tiles):
        upper = upper_ref[...].reshape(rows, DEPTH)
        lower = lower_ref[...].reshape(rows, DEPTH)
        parts = []
        for tile in tiles:
            mix = mix_ref[tile]
            part = jnp.dot(upper, mix, preferred_element_type=jnp.float32)
            parts.append(part + jnp.dot(lower, mix, preferred_element_type=jnp.float32))
        for spot in range(len(fold_bits)):
            size = rows >> (spot + 1)
            parts = [
                part[:size] + part[size:] * bits_ref[tile, spot:spot + 1, :] for part, tile in zip(parts, tiles)
            ]
        plane = len(fold_bits)
        return [part * bits_ref[tile, plane:plane + 1, :] for part, tile in zip(parts, tiles)]

    mine = me_chip * 2 + me_core

    def own_at(slot):
        @pl.when(me_core == 0)
        def _():
            recv_ref[mine] = send_ref[slot]

        @pl.when(me_core == 1)
        def _():
            recv_ref[mine] = send_ref[slot + 1]

    def start(slot, chip, core):
        pltpu.make_async_remote_copy(
            src_ref=send_ref.at[slot + core],
            dst_ref=recv_ref.at[mine],
            send_sem=send_sem,
            recv_sem=recv_sem,
            device_id=(jnp.right_shift(chip, inner_bits) * 2 + core, jnp.bitwise_and(chip, inner_count - 1)),
            device_id_type=MESH,
        ).start()

    def start_both(slot, chip, maybe_own):
        if not maybe_own:
            start(slot, chip, 0)
            start(slot, chip, 1)
            return
        own = chip == me_chip
        for core in range(2):
            @pl.when(jnp.logical_not(own & (me_core == core)))
            def _(core=core):
                start(slot, chip, core)

        @pl.when(own)
        def _():
            own_at(slot)

    def keep(slot, part):
        send_ref[slot] = part[:, :LANES]
        send_ref[slot + 1] = part[:, LANES:]

    plans = routes(far_count, side_count)

    def by_row(values):
        picked = values[0]
        for row, value in enumerate(values[1:], 1):
            if value != values[0]:
                picked = jnp.where(me_far == row, value, picked)
        return picked

    opened = [set() for _ in range(far_count)]
    relayed = False
    place = 0
    for size in GROUPS:
        chips = []
        for spot in range(place, place + size):
            far = by_row([plan[spot][0] for plan in plans])
            side = by_row([plan[spot][1] for plan in plans])
            swapped = side
            for row, plan in enumerate(plans):
                if LEADS[row] and plan[spot][0] == 0:
                    start_spot = min(index for index, one in enumerate(plan) if one[0] == 0)
                    value = me_side if spot == start_spot else jnp.where(side == me_side, plan[start_spot][1], side)
                    swapped = jnp.where(me_far == row, value, swapped)
            side = jnp.bitwise_xor(me_side, swapped)
            upper = jnp.right_shift(side, near_bits) * inner_count
            chips.append(upper + far * (1 << near_bits) + jnp.bitwise_and(side, (1 << near_bits) - 1))
        for spot, part in enumerate(parts_of(chips), place):
            keep(spot * 2, part)
        if not relayed:
            relayed = True

            @pl.when(me_core == 1)
            def _():
                pl.semaphore_wait(ready_sem.at[relay], 1)

        for far in range(far_count):
            fresh = []
            for row, plan in enumerate(plans):
                if far not in opened[row] and any(one == far for one, _ in plan[place:place + size]):
                    opened[row].add(far)
                    if far >= row:
                        fresh.append(row)
            for row in fresh:
                wanted = side_count if far > row else side_count - 1 - me_side

                @pl.when((me_far == row) & (wanted > 0))
                def _(far=far, wanted=wanted):
                    pl.semaphore_wait(ready_sem.at[far], wanted)
        for spot, chip in enumerate(chips, place):
            start_both(spot * 2, chip, any(plan[spot] == (row, 0) or (row == 0 and LEADS[0] and plan[spot][0] == 0) for row, plan in enumerate(plans)))
        place += size
    for swap in swaps:
        swap.wait_send()
    everything = pltpu.make_async_remote_copy(
        src_ref=send_ref.at[pl.ds(0, device_count - 1)],
        dst_ref=recv_ref.at[pl.ds(0, device_count - 1)],
        send_sem=send_sem,
        recv_sem=recv_sem,
        device_id=partner,
        device_id_type=MESH,
    )
    everything.wait_send()
    everything.wait_recv()
    for core in range(2):
        terms = [recv_ref[chip * 2 + core] for chip in range(chip_count)]
        while len(terms) > 1:
            terms = [one + other for one, other in zip(terms[::2], terms[1::2])]
        out_ref[core * half:(core + 1) * half, :] = terms[0]


def solution(mesh):
    outer_count, inner_count = mesh.shape["outer"], mesh.shape["inner"]
    device_count = outer_count * inner_count

    def local(matrix_panel, row_signs, kept_rows):
        columns, local_rows = matrix_panel.shape
        kept_count = kept_rows.shape[0]
        half = columns // 2
        powers = all(size & (size - 1) == 0 for size in (outer_count, inner_count, local_rows))
        fits = (
            powers
            and outer_count % 2 == 0
            and device_count >= 4
            and columns % (2 * PACK) == 0
            and kept_count == device_count * LANES
            and local_rows % (2 * DEPTH) == 0
        )
        if not fits:
            return scatter_form(matrix_panel, row_signs, kept_rows)
        mids = local_rows // DEPTH
        chips = device_count // 2
        arrived = pl.pallas_call(
            functools.partial(kernel, outer_count, inner_count, 1.0 / math.sqrt(local_rows * device_count)),
            out_shape=pltpu.VMEM((columns, LANES), jnp.float32),
            in_specs=[pl.BlockSpec(memory_space=pl.ANY)] * 3,
            out_specs=pl.BlockSpec(memory_space=pltpu.VMEM),
            scratch_shapes=[
                pltpu.VMEM((2, half, local_rows), jnp.float32),
                pltpu.VMEM((2, 1, local_rows), jnp.int32),
                pltpu.VMEM((1, kept_count), jnp.int32),
                pltpu.VMEM((2, mids * half, DEPTH), jnp.bfloat16),
                pltpu.VMEM((2, mids * half, DEPTH), jnp.bfloat16),
                pltpu.VMEM((chips, DEPTH, 2 * LANES), jnp.bfloat16),
                pltpu.VMEM((chips, 8, 2 * LANES), jnp.float32),
                pltpu.VMEM((device_count, half, LANES), jnp.float32),
                pltpu.VMEM((device_count, half, LANES), jnp.float32),
                pltpu.SemaphoreType.DMA((3,)),
                pltpu.SemaphoreType.DMA((2,)),
                pltpu.SemaphoreType.DMA((2,)),
                pltpu.SemaphoreType.DMA(()),
                pltpu.SemaphoreType.DMA(()),
                pltpu.SemaphoreType.REGULAR((max(inner_count // 2, 1) + 2,)),
            ],
            compiler_params=pltpu.CompilerParams(collective_id=0, has_side_effects=True),
        )(matrix_panel, row_signs.reshape(1, local_rows), kept_rows.reshape(1, kept_count))
        return arrived.T

    return jax.shard_map(
        local,
        mesh=mesh,
        in_specs=(P(None, ("outer", "inner")), P(("outer", "inner")), P()),
        out_specs=P(("outer", "inner"), None),
        check_vma=False,
    )
```

```python
import functools
import math

import jax
import jax.numpy as jnp
from jax import lax
from jax.experimental import pallas as pl
from jax.experimental.pallas import tpu as pltpu
from jax.sharding import PartitionSpec as P

MESH = pl.DeviceIdType.MESH
LANES = 128
DEPTH = 256
PACK = 16
GROUPS = [4, 4, 4, 4]
LEADS = [1, 1, 1, 1]
SETS = [[0, 0, 0, 0], [1, 1, 1, 1], [2, 2, 2, 2], [3, 3, 3, 3]]
WEIGHTS = [10, 20, 31, 60]
ROUTES = [[(0, 3), (0, 2), (0, 1), (0, 0), (1, 3), (1, 2), (1, 1), (1, 0), (2, 3), (2, 2), (2, 1), (2, 0), (3, 3), (3, 2), (3, 1), (3, 0)], [(0, 3), (0, 2), (0, 1), (0, 0), (2, 3), (2, 2), (2, 1), (2, 0), (1, 3), (1, 2), (1, 1), (1, 0), (3, 3), (3, 2), (3, 1), (3, 0)], [(0, 3), (0, 2), (0, 1), (0, 0), (1, 3), (1, 2), (1, 1), (1, 0), (3, 3), (3, 2), (3, 1), (3, 0), (2, 3), (2, 2), (2, 1), (2, 0)], [(0, 3), (0, 2), (0, 1), (0, 0), (1, 3), (1, 2), (1, 1), (1, 0), (3, 3), (3, 2), (3, 1), (3, 0), (2, 3), (2, 2), (2, 1), (2, 0)]]


def bit_parity(values):
    folded = jnp.bitwise_xor(values, jnp.right_shift(values, 16))
    folded = jnp.bitwise_xor(folded, jnp.right_shift(folded, 8))
    folded = jnp.bitwise_xor(folded, jnp.right_shift(folded, 4))
    folded = jnp.bitwise_xor(folded, jnp.right_shift(folded, 2))
    folded = jnp.bitwise_xor(folded, jnp.right_shift(folded, 1))
    return jnp.bitwise_and(folded, 1)


def hadamard(order_size):
    positions = lax.iota(jnp.int32, order_size)
    shared = jnp.bitwise_and(positions[:, None], positions[None, :])
    return jnp.where(bit_parity(shared) == 0, 1.0, -1.0).astype(jnp.float32)


def scatter_form(matrix_panel, row_signs, kept_rows):
    highest = lax.Precision.HIGHEST
    columns, local_rows = matrix_panel.shape
    outer_count = lax.axis_size("outer")
    inner_count = lax.axis_size("inner")
    device_count = outer_count * inner_count
    total_rows = local_rows * device_count
    me_outer = lax.axis_index("outer")
    me_inner = lax.axis_index("inner")
    signed = matrix_panel * row_signs.astype(jnp.float32)[None, :]
    leading = 128
    trailing = local_rows // leading
    blocks = signed.reshape(columns, leading, trailing)
    blocks = jnp.einsum("ap,jpq->jaq", hadamard(leading), blocks, precision=highest)
    blocks = jnp.einsum("bq,jaq->jab", hadamard(trailing), blocks, precision=highest)
    local_mix = blocks.reshape(columns, local_rows)
    low_bits = kept_rows % local_rows
    high_outer = kept_rows // (local_rows * inner_count)
    high_inner = kept_rows // local_rows % inner_count
    flips = bit_parity(jnp.bitwise_and(high_outer, me_outer)) + bit_parity(
        jnp.bitwise_and(high_inner, me_inner)
    )
    parity_sign = jnp.where(flips % 2 == 0, 1.0, -1.0).astype(jnp.float32)
    values = jnp.take(local_mix, low_bits, axis=1)
    summed = lax.psum_scatter(
        (values * parity_sign[None, :]).T, ("outer", "inner"), scatter_dimension=0, tiled=True
    )
    return summed * (1.0 / math.sqrt(total_rows))


def log2(size):
    return size.bit_length() - 1


def sign_of_bit(rows, bit):
    return (1 - 2 * jnp.bitwise_and(jnp.right_shift(rows, bit), 1)).astype(jnp.float32)


def bit_of(index, bit):
    return jnp.bitwise_and(jnp.right_shift(index, bit), 1)


def routes(far_count, side_count):
    if far_count == 4 and side_count == 4:
        return ROUTES
    return [[(far, side) for far in range(far_count) for side in reversed(range(side_count))] for _ in range(far_count)]


def ready_sets(far_count, side_count):
    if far_count == 4 and side_count == 4:
        return SETS
    return [[far] * side_count for far in range(far_count)]


def key_weights(side_bits, far_bits):
    if side_bits == 2 and far_bits == 2:
        return WEIGHTS
    return [1 << bit for bit in range(side_bits + far_bits)]


def kernel(
    outer_count, inner_count, scale,
    panel_hbm, signs_hbm, kept_hbm, out_ref,
    panel_ref, signs_ref, kept_ref, upper_ref, lower_ref, mix_ref, bits_ref, send_ref, recv_ref,
    load_sem, swap_send, swap_recv, send_sem, recv_sem, ready_sem,
):
    device_count = outer_count * inner_count
    chip_count = device_count // 2
    chip_bits = log2(chip_count)
    inner_bits = log2(inner_count)
    near_bits = min(1, inner_bits)
    far_bits = inner_bits - near_bits
    far_count = 1 << far_bits
    side_bits = chip_bits - far_bits
    side_count = 1 << side_bits
    columns, local_rows = panel_hbm.shape
    half = columns // 2
    mids = local_rows // DEPTH
    rows = 2 * mids * half
    me_outer = lax.axis_index("outer")
    me_inner = lax.axis_index("inner")
    me_core = bit_of(me_outer, 0)
    me_chip = jnp.right_shift(me_outer, 1) * inner_count + me_inner
    me_far = jnp.right_shift(me_inner, near_bits)
    me_side = jnp.right_shift(me_outer, 1) * (1 << near_bits) + jnp.bitwise_and(me_inner, (1 << near_bits) - 1)
    partner = (jnp.bitwise_xor(me_outer, 1), me_inner)

    own_rows = pl.ds(pl.multiple_of(me_core * half, half), half)
    other_rows = pl.ds(pl.multiple_of((1 - me_core) * half, half), half)
    loads = [
        pltpu.make_async_copy(source, target, load_sem.at[spot])
        for spot, (source, target) in enumerate(
            [
                (kept_hbm, kept_ref),
                (signs_hbm, signs_ref.at[me_core]),
                (panel_hbm.at[own_rows, :], panel_ref.at[me_core]),
            ]
        )
    ]

    for load in loads:
        load.start()

    weights = key_weights(side_bits, far_bits)
    sets = ready_sets(far_count, side_count)
    set_count = 1 + max(max(row) for row in sets)

    def key_of(far, side):
        bits = [side >> bit & 1 for bit in range(side_bits)] + [far >> bit & 1 for bit in range(far_bits)]
        return sum(weight * bit for weight, bit in zip(weights, bits))

    chips_by_key = sorted((key_of(far, side), far, side) for far in range(far_count) for side in range(side_count))
    me_key = 0
    for bit in range(side_bits):
        me_key = me_key + weights[bit] * bit_of(me_side, bit)
    for bit in range(far_bits):
        me_key = me_key + weights[side_bits + bit] * bit_of(me_far, bit)
    me_set = 0
    for far in range(far_count):
        for side in range(side_count):
            if sets[far][side]:
                me_set = jnp.where((me_far == far) & (me_side == side), sets[far][side], me_set)
    earlier = 0
    for key, _, _ in chips_by_key:
        earlier = earlier + jnp.where(key < me_key, 1, 0)
    pair, relay = set_count, set_count + 1

    def at(far, side, core):
        near = side & ((1 << near_bits) - 1)
        return ((side >> near_bits) * 2 + core, (far << near_bits) + near)

    def tell(semaphore, device):
        pl.semaphore_signal(semaphore, inc=1, device_id=device, device_id_type=MESH)

    barrier = pltpu.get_barrier_semaphore()

    @pl.when(me_core == 0)
    def _():
        tell(barrier, partner)

    for key, far, side in reversed(chips_by_key):
        @pl.when(me_key < key)
        def _(far=far, side=side):
            tell(barrier, at(far, side, 0))

    swaps = [
        pltpu.make_async_remote_copy(
            src_ref=source, dst_ref=target, send_sem=swap_send.at[spot], recv_sem=swap_recv.at[spot],
            device_id=partner, device_id_type=MESH,
        )
        for spot, (source, target) in enumerate(
            [(signs_hbm, signs_ref.at[me_core]), (panel_hbm.at[other_rows, :], panel_ref.at[me_core])]
        )
    ]

    @pl.when(me_core == 1)
    def _():
        pl.semaphore_wait(barrier, 1)
        tell(ready_sem.at[pair], partner)

    @pl.when(me_core == 0)
    def _():
        pl.semaphore_wait(ready_sem.at[pair], 1)

    for swap in swaps:
        swap.start()

    def settle():
        @pl.when(earlier > 0)
        def _():
            pl.semaphore_wait(barrier, 2 * earlier)

        tell(ready_sem.at[relay], partner)
        for key, far, side in chips_by_key:
            @pl.when(me_key > key)
            def _(far=far, side=side):
                for core in range(2):
                    tell(ready_sem.at[me_set], at(far, side, core))

    @pl.when((me_core == 0) & (me_side == side_count - 1))
    def _():
        settle()

    core_bit = log2(local_rows) + inner_bits
    chip_at = [log2(local_rows) + bit for bit in range(inner_bits)]
    chip_at += [core_bit + 1 + bit for bit in range(chip_bits - inner_bits)]
    fold_bits = [core_bit] + [bit for bit in reversed(range(log2(DEPTH), log2(local_rows)))]

    loads[0].wait()

    def signs_of(tile, carry):
        first = jnp.right_shift(tile, inner_bits) * 2 * inner_count + jnp.bitwise_and(tile, inner_count - 1)
        kept = jnp.concatenate(
            [
                kept_ref[:, pl.ds(pl.multiple_of(block * LANES, LANES), LANES)]
                for block in (first, first + inner_count)
            ],
            axis=1,
        )
        width = 2 * LANES
        for spot, bit in enumerate(fold_bits):
            bits_ref[tile, spot:spot + 1, :] = sign_of_bit(kept, bit)
        plane = jnp.full((1, width), scale, jnp.float32)
        for bit, position in enumerate(chip_at):
            plane = plane * jnp.where(bit_of(me_chip, bit) == 1, sign_of_bit(kept, position), 1.0)
        bits_ref[tile, len(fold_bits):len(fold_bits) + 1, :] = plane
        position = lax.broadcasted_iota(jnp.int32, (PACK, width), 0)
        base = jnp.ones((PACK, width), jnp.float32)
        for bit in range(log2(PACK)):
            taken = jnp.bitwise_and(jnp.right_shift(position, bit), 1) == 1
            base = base * jnp.where(taken, sign_of_bit(kept, bit), 1.0)
        blocks = [base.astype(jnp.bfloat16)]
        for bit in range(log2(PACK), log2(DEPTH)):
            flip = jnp.broadcast_to(sign_of_bit(kept, bit), (PACK, width)).astype(jnp.bfloat16)
            blocks = blocks + [block * flip for block in blocks]
        for top, block in enumerate(blocks):
            mix_ref[tile, top * PACK:(top + 1) * PACK, :] = block
        return carry

    lax.fori_loop(0, chip_count, signs_of, 0)

    @pl.when((me_core == 0) & (me_side > 0) & (me_side < side_count - 1))
    def _():
        settle()


    def split(core):
        for mid in range(mids):
            lanes = slice(mid * DEPTH, (mid + 1) * DEPTH)
            block = panel_ref[core, :, lanes] * signs_ref[core, :, lanes].astype(jnp.float32)
            upper = block.astype(jnp.bfloat16)
            lower = (block - upper.astype(jnp.float32)).astype(jnp.bfloat16)
            upper_ref[core, mid * half:(mid + 1) * half, :] = upper
            lower_ref[core, mid * half:(mid + 1) * half, :] = lower

    for load in loads[1:]:
        load.wait()
    split(me_core)
    for swap in swaps:
        swap.wait_recv()
    split(1 - me_core)

    def parts_of(tiles):
        upper = upper_ref[...].reshape(rows, DEPTH)
        lower = lower_ref[...].reshape(rows, DEPTH)
        parts = []
        for tile in tiles:
            mix = mix_ref[tile]
            part = jnp.dot(upper, mix, preferred_element_type=jnp.float32)
            parts.append(part + jnp.dot(lower, mix, preferred_element_type=jnp.float32))
        for spot in range(len(fold_bits)):
            size = rows >> (spot + 1)
            parts = [
                part[:size] + part[size:] * bits_ref[tile, spot:spot + 1, :] for part, tile in zip(parts, tiles)
            ]
        plane = len(fold_bits)
        return [part * bits_ref[tile, plane:plane + 1, :] for part, tile in zip(parts, tiles)]

    mine = me_chip * 2 + me_core

    def own_at(slot):
        @pl.when(me_core == 0)
        def _():
            recv_ref[mine] = send_ref[slot]

        @pl.when(me_core == 1)
        def _():
            recv_ref[mine] = send_ref[slot + 1]

    def start(slot, chip, core):
        pltpu.make_async_remote_copy(
            src_ref=send_ref.at[slot + core],
            dst_ref=recv_ref.at[mine],
            send_sem=send_sem,
            recv_sem=recv_sem,
            device_id=(jnp.right_shift(chip, inner_bits) * 2 + core, jnp.bitwise_and(chip, inner_count - 1)),
            device_id_type=MESH,
        ).start()

    def start_both(slot, chip, maybe_own):
        if not maybe_own:
            start(slot, chip, 0)
            start(slot, chip, 1)
            return
        own = chip == me_chip
        for core in range(2):
            @pl.when(jnp.logical_not(own & (me_core == core)))
            def _(core=core):
                start(slot, chip, core)

        @pl.when(own)
        def _():
            own_at(slot)

    def keep(slot, part):
        send_ref[slot] = part[:, :LANES]
        send_ref[slot + 1] = part[:, LANES:]

    plans = routes(far_count, side_count)

    def by_row(values):
        picked = values[0]
        for row, value in enumerate(values[1:], 1):
            if value != values[0]:
                picked = jnp.where(me_far == row, value, picked)
        return picked

    def waited(chosen):
        total = 0
        for key, far, side in chips_by_key:
            if sets[far][side] == chosen:
                total = total + jnp.where(key > me_key, 1, 0)
        return total

    wanted = [waited(chosen) for chosen in range(set_count)]
    opened = [set() for _ in range(far_count)]
    place = 0
    for size in GROUPS if chip_count == sum(GROUPS) else [1] * chip_count:
        chips = []
        for spot in range(place, place + size):
            far = by_row([plan[spot][0] for plan in plans])
            swapped = by_row([plan[spot][1] % side_count for plan in plans])
            for row, plan in enumerate(plans):
                value = None
                if LEADS[row % len(LEADS)] and plan[spot][0] == 0:
                    start_spot = min(index for index, one in enumerate(plan) if one[0] == 0)
                    lead = plan[start_spot][1]
                    value = me_side if spot == start_spot else jnp.where(swapped == me_side, lead, swapped)
                elif plan[spot][1] >= side_count:
                    value = jnp.bitwise_xor(me_side, plan[spot][1] - side_count)
                if value is not None:
                    swapped = jnp.where(me_far == row, value, swapped)
            side = jnp.bitwise_xor(me_side, swapped)
            upper = jnp.right_shift(side, near_bits) * inner_count
            chips.append(upper + far * (1 << near_bits) + jnp.bitwise_and(side, (1 << near_bits) - 1))
        for spot, part in enumerate(parts_of(chips), place):
            keep(spot * 2, part)
        if place == 0:
            @pl.when((me_core == 0) & (me_side == 0))
            def _():
                settle()

            @pl.when(me_core == 1)
            def _():
                pl.semaphore_wait(ready_sem.at[relay], 1)

        for spot, chip in enumerate(chips, place):
            fresh = {}
            for row, plan in enumerate(plans):
                far, side = plan[spot]
                reached = [sets[far][side - side_count]] if side >= side_count else sets[far]
                for chosen in sorted(set(reached) - opened[row]):
                    opened[row].add(chosen)
                    fresh.setdefault(chosen, []).append(row)
            for chosen, opening in fresh.items():
                here = me_far == opening[0]
                for row in opening[1:]:
                    here = here | (me_far == row)

                @pl.when(here & (wanted[chosen] > 0))
                def _(chosen=chosen):
                    pl.semaphore_wait(ready_sem.at[chosen], wanted[chosen])

            own = any(
                plan[spot][0] == row and (plan[spot][1] % side_count == 0 or plan[spot][1] >= side_count or row == 0)
                for row, plan in enumerate(plans)
            )
            start_both(spot * 2, chip, own)
        place += size
    for swap in swaps:
        swap.wait_send()
    everything = pltpu.make_async_remote_copy(
        src_ref=send_ref.at[pl.ds(0, device_count - 1)],
        dst_ref=recv_ref.at[pl.ds(0, device_count - 1)],
        send_sem=send_sem,
        recv_sem=recv_sem,
        device_id=partner,
        device_id_type=MESH,
    )
    everything.wait_send()
    everything.wait_recv()
    for core in range(2):
        terms = [recv_ref[chip * 2 + core] for chip in range(chip_count)]
        while len(terms) > 1:
            terms = [one + other for one, other in zip(terms[::2], terms[1::2])]
        out_ref[core * half:(core + 1) * half, :] = terms[0]


def solution(mesh):
    outer_count, inner_count = mesh.shape["outer"], mesh.shape["inner"]
    device_count = outer_count * inner_count

    def local(matrix_panel, row_signs, kept_rows):
        columns, local_rows = matrix_panel.shape
        kept_count = kept_rows.shape[0]
        half = columns // 2
        powers = all(size & (size - 1) == 0 for size in (outer_count, inner_count, local_rows))
        fits = (
            powers
            and outer_count % 2 == 0
            and device_count >= 4
            and columns % (2 * PACK) == 0
            and kept_count == device_count * LANES
            and local_rows % (2 * DEPTH) == 0
        )
        if not fits:
            return scatter_form(matrix_panel, row_signs, kept_rows)
        mids = local_rows // DEPTH
        chips = device_count // 2
        arrived = pl.pallas_call(
            functools.partial(kernel, outer_count, inner_count, 1.0 / math.sqrt(local_rows * device_count)),
            out_shape=pltpu.VMEM((columns, LANES), jnp.float32),
            in_specs=[pl.BlockSpec(memory_space=pl.ANY)] * 3,
            out_specs=pl.BlockSpec(memory_space=pltpu.VMEM),
            scratch_shapes=[
                pltpu.VMEM((2, half, local_rows), jnp.float32),
                pltpu.VMEM((2, 1, local_rows), jnp.int32),
                pltpu.VMEM((1, kept_count), jnp.int32),
                pltpu.VMEM((2, mids * half, DEPTH), jnp.bfloat16),
                pltpu.VMEM((2, mids * half, DEPTH), jnp.bfloat16),
                pltpu.VMEM((chips, DEPTH, 2 * LANES), jnp.bfloat16),
                pltpu.VMEM((chips, 8, 2 * LANES), jnp.float32),
                pltpu.VMEM((device_count, half, LANES), jnp.float32),
                pltpu.VMEM((device_count, half, LANES), jnp.float32),
                pltpu.SemaphoreType.DMA((3,)),
                pltpu.SemaphoreType.DMA((2,)),
                pltpu.SemaphoreType.DMA((2,)),
                pltpu.SemaphoreType.DMA(()),
                pltpu.SemaphoreType.DMA(()),
                pltpu.SemaphoreType.REGULAR((max(inner_count // 2, 4) + 2,)),
            ],
            compiler_params=pltpu.CompilerParams(collective_id=0, has_side_effects=True),
        )(matrix_panel, row_signs.reshape(1, local_rows), kept_rows.reshape(1, kept_count))
        return arrived.T

    return jax.shard_map(
        local,
        mesh=mesh,
        in_specs=(P(None, ("outer", "inner")), P(("outer", "inner")), P()),
        out_specs=P(("outer", "inner"), None),
        check_vma=False,
    )
```

```python
import functools
import math

import jax
import jax.numpy as jnp
from jax import lax
from jax.experimental import pallas as pl
from jax.experimental.pallas import tpu as pltpu
from jax.sharding import PartitionSpec as P

MESH = pl.DeviceIdType.MESH
LANES = 128
DEPTH = 256
PACK = 16
GROUPS = [2, 6, 4, 4]
LEADS = [1, 1, 1, 1]
SETS = [[0, 0, 0, 0], [1, 1, 1, 1], [2, 2, 2, 2], [4, 3, 3, 3]]
WEIGHTS = [10, 20, 31, 60]
ROUTES = [[(0, 3), (0, 2), (0, 1), (0, 0), (1, 3), (1, 2), (1, 1), (1, 0), (2, 3), (2, 2), (2, 1), (2, 0), (3, 3), (3, 2), (3, 1), (3, 0)], [(0, 3), (0, 2), (0, 1), (0, 0), (2, 3), (2, 2), (2, 1), (2, 0), (1, 3), (1, 2), (1, 1), (1, 0), (3, 4), (3, 6), (3, 5), (3, 7)], [(0, 3), (0, 2), (0, 1), (0, 0), (1, 3), (1, 2), (1, 1), (1, 0), (3, 3), (3, 2), (3, 1), (3, 0), (2, 3), (2, 2), (2, 1), (2, 0)], [(0, 3), (0, 2), (0, 1), (0, 0), (1, 3), (1, 2), (1, 1), (1, 0), (3, 3), (3, 2), (3, 1), (3, 0), (2, 3), (2, 2), (2, 1), (2, 0)]]


def bit_parity(values):
    folded = jnp.bitwise_xor(values, jnp.right_shift(values, 16))
    folded = jnp.bitwise_xor(folded, jnp.right_shift(folded, 8))
    folded = jnp.bitwise_xor(folded, jnp.right_shift(folded, 4))
    folded = jnp.bitwise_xor(folded, jnp.right_shift(folded, 2))
    folded = jnp.bitwise_xor(folded, jnp.right_shift(folded, 1))
    return jnp.bitwise_and(folded, 1)


def hadamard(order_size):
    positions = lax.iota(jnp.int32, order_size)
    shared = jnp.bitwise_and(positions[:, None], positions[None, :])
    return jnp.where(bit_parity(shared) == 0, 1.0, -1.0).astype(jnp.float32)


def scatter_form(matrix_panel, row_signs, kept_rows):
    highest = lax.Precision.HIGHEST
    columns, local_rows = matrix_panel.shape
    outer_count = lax.axis_size("outer")
    inner_count = lax.axis_size("inner")
    device_count = outer_count * inner_count
    total_rows = local_rows * device_count
    me_outer = lax.axis_index("outer")
    me_inner = lax.axis_index("inner")
    signed = matrix_panel * row_signs.astype(jnp.float32)[None, :]
    leading = 128
    trailing = local_rows // leading
    blocks = signed.reshape(columns, leading, trailing)
    blocks = jnp.einsum("ap,jpq->jaq", hadamard(leading), blocks, precision=highest)
    blocks = jnp.einsum("bq,jaq->jab", hadamard(trailing), blocks, precision=highest)
    local_mix = blocks.reshape(columns, local_rows)
    low_bits = kept_rows % local_rows
    high_outer = kept_rows // (local_rows * inner_count)
    high_inner = kept_rows // local_rows % inner_count
    flips = bit_parity(jnp.bitwise_and(high_outer, me_outer)) + bit_parity(
        jnp.bitwise_and(high_inner, me_inner)
    )
    parity_sign = jnp.where(flips % 2 == 0, 1.0, -1.0).astype(jnp.float32)
    values = jnp.take(local_mix, low_bits, axis=1)
    summed = lax.psum_scatter(
        (values * parity_sign[None, :]).T, ("outer", "inner"), scatter_dimension=0, tiled=True
    )
    return summed * (1.0 / math.sqrt(total_rows))


def log2(size):
    return size.bit_length() - 1


def sign_of_bit(rows, bit):
    return (1 - 2 * jnp.bitwise_and(jnp.right_shift(rows, bit), 1)).astype(jnp.float32)


def bit_of(index, bit):
    return jnp.bitwise_and(jnp.right_shift(index, bit), 1)


def routes(far_count, side_count):
    if far_count == 4 and side_count == 4:
        return ROUTES
    return [[(far, side) for far in range(far_count) for side in reversed(range(side_count))] for _ in range(far_count)]


def ready_sets(far_count, side_count):
    if far_count == 4 and side_count == 4:
        return SETS
    return [[far] * side_count for far in range(far_count)]


def key_weights(side_bits, far_bits):
    if side_bits == 2 and far_bits == 2:
        return WEIGHTS
    return [1 << bit for bit in range(side_bits + far_bits)]


def kernel(
    outer_count, inner_count, scale,
    panel_hbm, signs_hbm, kept_hbm, out_ref,
    panel_ref, signs_ref, kept_ref, upper_ref, lower_ref, mix_ref, bits_ref, send_ref, recv_ref,
    load_sem, swap_send, swap_recv, send_sem, recv_sem, ready_sem,
):
    device_count = outer_count * inner_count
    chip_count = device_count // 2
    chip_bits = log2(chip_count)
    inner_bits = log2(inner_count)
    near_bits = min(1, inner_bits)
    far_bits = inner_bits - near_bits
    far_count = 1 << far_bits
    side_bits = chip_bits - far_bits
    side_count = 1 << side_bits
    columns, local_rows = panel_hbm.shape
    half = columns // 2
    mids = local_rows // DEPTH
    rows = 2 * mids * half
    me_outer = lax.axis_index("outer")
    me_inner = lax.axis_index("inner")
    me_core = bit_of(me_outer, 0)
    me_chip = jnp.right_shift(me_outer, 1) * inner_count + me_inner
    me_far = jnp.right_shift(me_inner, near_bits)
    me_side = jnp.right_shift(me_outer, 1) * (1 << near_bits) + jnp.bitwise_and(me_inner, (1 << near_bits) - 1)
    partner = (jnp.bitwise_xor(me_outer, 1), me_inner)

    own_rows = pl.ds(pl.multiple_of(me_core * half, half), half)
    other_rows = pl.ds(pl.multiple_of((1 - me_core) * half, half), half)
    loads = [
        pltpu.make_async_copy(source, target, load_sem.at[spot])
        for spot, (source, target) in enumerate(
            [
                (kept_hbm, kept_ref),
                (signs_hbm, signs_ref.at[me_core]),
                (panel_hbm.at[own_rows, :], panel_ref.at[me_core]),
            ]
        )
    ]

    for load in loads:
        load.start()

    weights = key_weights(side_bits, far_bits)
    sets = ready_sets(far_count, side_count)
    set_count = 1 + max(max(row) for row in sets)

    def key_of(far, side):
        bits = [side >> bit & 1 for bit in range(side_bits)] + [far >> bit & 1 for bit in range(far_bits)]
        return sum(weight * bit for weight, bit in zip(weights, bits))

    chips_by_key = sorted((key_of(far, side), far, side) for far in range(far_count) for side in range(side_count))
    me_key = 0
    for bit in range(side_bits):
        me_key = me_key + weights[bit] * bit_of(me_side, bit)
    for bit in range(far_bits):
        me_key = me_key + weights[side_bits + bit] * bit_of(me_far, bit)
    me_set = 0
    for far in range(far_count):
        for side in range(side_count):
            if sets[far][side]:
                me_set = jnp.where((me_far == far) & (me_side == side), sets[far][side], me_set)
    earlier = 0
    for key, _, _ in chips_by_key:
        earlier = earlier + jnp.where(key < me_key, 1, 0)
    pair, relay = set_count, set_count + 1

    def at(far, side, core):
        near = side & ((1 << near_bits) - 1)
        return ((side >> near_bits) * 2 + core, (far << near_bits) + near)

    def tell(semaphore, device):
        pl.semaphore_signal(semaphore, inc=1, device_id=device, device_id_type=MESH)

    barrier = pltpu.get_barrier_semaphore()

    @pl.when(me_core == 0)
    def _():
        tell(barrier, partner)

    for key, far, side in reversed(chips_by_key):
        @pl.when(me_key < key)
        def _(far=far, side=side):
            tell(barrier, at(far, side, 0))

    swaps = [
        pltpu.make_async_remote_copy(
            src_ref=source, dst_ref=target, send_sem=swap_send.at[spot], recv_sem=swap_recv.at[spot],
            device_id=partner, device_id_type=MESH,
        )
        for spot, (source, target) in enumerate(
            [(signs_hbm, signs_ref.at[me_core]), (panel_hbm.at[other_rows, :], panel_ref.at[me_core])]
        )
    ]

    @pl.when(me_core == 1)
    def _():
        pl.semaphore_wait(barrier, 1)
        tell(ready_sem.at[pair], partner)

    @pl.when(me_core == 0)
    def _():
        pl.semaphore_wait(ready_sem.at[pair], 1)

    for swap in swaps:
        swap.start()

    def settle():
        @pl.when(earlier > 0)
        def _():
            pl.semaphore_wait(barrier, 2 * earlier)

        tell(ready_sem.at[relay], partner)
        for key, far, side in chips_by_key:
            @pl.when(me_key > key)
            def _(far=far, side=side):
                for core in range(2):
                    tell(ready_sem.at[me_set], at(far, side, core))

    @pl.when((me_core == 0) & (me_side == side_count - 1))
    def _():
        settle()

    core_bit = log2(local_rows) + inner_bits
    chip_at = [log2(local_rows) + bit for bit in range(inner_bits)]
    chip_at += [core_bit + 1 + bit for bit in range(chip_bits - inner_bits)]
    fold_bits = [core_bit] + [bit for bit in reversed(range(log2(DEPTH), log2(local_rows)))]

    loads[0].wait()

    def signs_of(tile, carry):
        first = jnp.right_shift(tile, inner_bits) * 2 * inner_count + jnp.bitwise_and(tile, inner_count - 1)
        kept = jnp.concatenate(
            [
                kept_ref[:, pl.ds(pl.multiple_of(block * LANES, LANES), LANES)]
                for block in (first, first + inner_count)
            ],
            axis=1,
        )
        width = 2 * LANES
        for spot, bit in enumerate(fold_bits):
            bits_ref[tile, spot:spot + 1, :] = sign_of_bit(kept, bit)
        plane = jnp.full((1, width), scale, jnp.float32)
        for bit, position in enumerate(chip_at):
            plane = plane * jnp.where(bit_of(me_chip, bit) == 1, sign_of_bit(kept, position), 1.0)
        bits_ref[tile, len(fold_bits):len(fold_bits) + 1, :] = plane
        position = lax.broadcasted_iota(jnp.int32, (PACK, width), 0)
        base = jnp.ones((PACK, width), jnp.float32)
        for bit in range(log2(PACK)):
            taken = jnp.bitwise_and(jnp.right_shift(position, bit), 1) == 1
            base = base * jnp.where(taken, sign_of_bit(kept, bit), 1.0)
        blocks = [base.astype(jnp.bfloat16)]
        for bit in range(log2(PACK), log2(DEPTH)):
            flip = jnp.broadcast_to(sign_of_bit(kept, bit), (PACK, width)).astype(jnp.bfloat16)
            blocks = blocks + [block * flip for block in blocks]
        for top, block in enumerate(blocks):
            mix_ref[tile, top * PACK:(top + 1) * PACK, :] = block
        return carry

    lax.fori_loop(0, chip_count, signs_of, 0)

    @pl.when((me_core == 0) & (me_side > 0) & (me_side < side_count - 1))
    def _():
        settle()


    def split(core):
        for mid in range(mids):
            lanes = slice(mid * DEPTH, (mid + 1) * DEPTH)
            block = panel_ref[core, :, lanes] * signs_ref[core, :, lanes].astype(jnp.float32)
            upper = block.astype(jnp.bfloat16)
            lower = (block - upper.astype(jnp.float32)).astype(jnp.bfloat16)
            upper_ref[core, mid * half:(mid + 1) * half, :] = upper
            lower_ref[core, mid * half:(mid + 1) * half, :] = lower

    for load in loads[1:]:
        load.wait()
    split(me_core)
    for swap in swaps:
        swap.wait_recv()
    split(1 - me_core)

    def parts_of(tiles):
        upper = upper_ref[...].reshape(rows, DEPTH)
        lower = lower_ref[...].reshape(rows, DEPTH)
        parts = []
        for tile in tiles:
            mix = mix_ref[tile]
            part = jnp.dot(upper, mix, preferred_element_type=jnp.float32)
            parts.append(part + jnp.dot(lower, mix, preferred_element_type=jnp.float32))
        for spot in range(len(fold_bits)):
            size = rows >> (spot + 1)
            parts = [
                part[:size] + part[size:] * bits_ref[tile, spot:spot + 1, :] for part, tile in zip(parts, tiles)
            ]
        plane = len(fold_bits)
        return [part * bits_ref[tile, plane:plane + 1, :] for part, tile in zip(parts, tiles)]

    mine = me_chip * 2 + me_core

    def own_at(slot):
        @pl.when(me_core == 0)
        def _():
            recv_ref[mine] = send_ref[slot]

        @pl.when(me_core == 1)
        def _():
            recv_ref[mine] = send_ref[slot + 1]

    def start(slot, chip, core):
        pltpu.make_async_remote_copy(
            src_ref=send_ref.at[slot + core],
            dst_ref=recv_ref.at[mine],
            send_sem=send_sem,
            recv_sem=recv_sem,
            device_id=(jnp.right_shift(chip, inner_bits) * 2 + core, jnp.bitwise_and(chip, inner_count - 1)),
            device_id_type=MESH,
        ).start()

    def start_both(slot, chip, maybe_own):
        cores = (0, 1) if slot == 0 else (1, 0)
        if not maybe_own:
            for core in cores:
                start(slot, chip, core)
            return
        own = chip == me_chip
        for core in cores:
            @pl.when(jnp.logical_not(own & (me_core == core)))
            def _(core=core):
                start(slot, chip, core)

        @pl.when(own)
        def _():
            own_at(slot)

    def keep(slot, part):
        send_ref[slot] = part[:, :LANES]
        send_ref[slot + 1] = part[:, LANES:]

    plans = routes(far_count, side_count)

    def by_row(values):
        picked = values[0]
        for row, value in enumerate(values[1:], 1):
            if value != values[0]:
                picked = jnp.where(me_far == row, value, picked)
        return picked

    def waited(chosen):
        total = 0
        for key, far, side in chips_by_key:
            if sets[far][side] == chosen:
                total = total + jnp.where(key > me_key, 1, 0)
        return total

    wanted = [waited(chosen) for chosen in range(set_count)]
    opened = [set() for _ in range(far_count)]
    place = 0
    for size in GROUPS if chip_count == sum(GROUPS) else [1] * chip_count:
        chips = []
        for spot in range(place, place + size):
            far = by_row([plan[spot][0] for plan in plans])
            swapped = by_row([plan[spot][1] % side_count for plan in plans])
            for row, plan in enumerate(plans):
                value = None
                if LEADS[row % len(LEADS)] and plan[spot][0] == 0:
                    start_spot = min(index for index, one in enumerate(plan) if one[0] == 0)
                    lead = plan[start_spot][1]
                    value = me_side if spot == start_spot else jnp.where(swapped == me_side, lead, swapped)
                elif plan[spot][1] >= side_count:
                    value = jnp.bitwise_xor(me_side, plan[spot][1] - side_count)
                if value is not None:
                    swapped = jnp.where(me_far == row, value, swapped)
            side = jnp.bitwise_xor(me_side, swapped)
            upper = jnp.right_shift(side, near_bits) * inner_count
            chips.append(upper + far * (1 << near_bits) + jnp.bitwise_and(side, (1 << near_bits) - 1))
        for spot, part in enumerate(parts_of(chips), place):
            keep(spot * 2, part)
        if place == 0:
            @pl.when((me_core == 0) & (me_side == 0))
            def _():
                settle()

            @pl.when(me_core == 1)
            def _():
                pl.semaphore_wait(ready_sem.at[relay], 1)

        for spot, chip in enumerate(chips, place):
            fresh = {}
            for row, plan in enumerate(plans):
                far, side = plan[spot]
                reached = [sets[far][side - side_count]] if side >= side_count else sets[far]
                for chosen in sorted(set(reached) - opened[row]):
                    opened[row].add(chosen)
                    fresh.setdefault(chosen, []).append(row)
            for chosen, opening in fresh.items():
                here = me_far == opening[0]
                for row in opening[1:]:
                    here = here | (me_far == row)

                @pl.when(here & (wanted[chosen] > 0))
                def _(chosen=chosen):
                    pl.semaphore_wait(ready_sem.at[chosen], wanted[chosen])

            own = any(
                plan[spot][0] == row and (plan[spot][1] % side_count == 0 or plan[spot][1] >= side_count or row == 0)
                for row, plan in enumerate(plans)
            )
            start_both(spot * 2, chip, own)
        place += size
    for swap in swaps:
        swap.wait_send()
    everything = pltpu.make_async_remote_copy(
        src_ref=send_ref.at[pl.ds(0, device_count - 1)],
        dst_ref=recv_ref.at[pl.ds(0, device_count - 1)],
        send_sem=send_sem,
        recv_sem=recv_sem,
        device_id=partner,
        device_id_type=MESH,
    )
    everything.wait_send()
    everything.wait_recv()
    for core in range(2):
        terms = [recv_ref[chip * 2 + core] for chip in range(chip_count)]
        while len(terms) > 1:
            terms = [one + other for one, other in zip(terms[::2], terms[1::2])]
        out_ref[core * half:(core + 1) * half, :] = terms[0]


def solution(mesh):
    outer_count, inner_count = mesh.shape["outer"], mesh.shape["inner"]
    device_count = outer_count * inner_count

    def local(matrix_panel, row_signs, kept_rows):
        columns, local_rows = matrix_panel.shape
        kept_count = kept_rows.shape[0]
        half = columns // 2
        powers = all(size & (size - 1) == 0 for size in (outer_count, inner_count, local_rows))
        fits = (
            powers
            and outer_count % 2 == 0
            and device_count >= 4
            and columns % (2 * PACK) == 0
            and kept_count == device_count * LANES
            and local_rows % (2 * DEPTH) == 0
        )
        if not fits:
            return scatter_form(matrix_panel, row_signs, kept_rows)
        mids = local_rows // DEPTH
        chips = device_count // 2
        arrived = pl.pallas_call(
            functools.partial(kernel, outer_count, inner_count, 1.0 / math.sqrt(local_rows * device_count)),
            out_shape=pltpu.VMEM((columns, LANES), jnp.float32),
            in_specs=[pl.BlockSpec(memory_space=pl.ANY)] * 3,
            out_specs=pl.BlockSpec(memory_space=pltpu.VMEM),
            scratch_shapes=[
                pltpu.VMEM((2, half, local_rows), jnp.float32),
                pltpu.VMEM((2, 1, local_rows), jnp.int32),
                pltpu.VMEM((1, kept_count), jnp.int32),
                pltpu.VMEM((2, mids * half, DEPTH), jnp.bfloat16),
                pltpu.VMEM((2, mids * half, DEPTH), jnp.bfloat16),
                pltpu.VMEM((chips, DEPTH, 2 * LANES), jnp.bfloat16),
                pltpu.VMEM((chips, 8, 2 * LANES), jnp.float32),
                pltpu.VMEM((device_count, half, LANES), jnp.float32),
                pltpu.VMEM((device_count, half, LANES), jnp.float32),
                pltpu.SemaphoreType.DMA((3,)),
                pltpu.SemaphoreType.DMA((2,)),
                pltpu.SemaphoreType.DMA((2,)),
                pltpu.SemaphoreType.DMA(()),
                pltpu.SemaphoreType.DMA(()),
                pltpu.SemaphoreType.REGULAR((max(inner_count // 2 + 2, 8),)),
            ],
            compiler_params=pltpu.CompilerParams(collective_id=0, has_side_effects=True),
        )(matrix_panel, row_signs.reshape(1, local_rows), kept_rows.reshape(1, kept_count))
        return arrived.T

    return jax.shard_map(
        local,
        mesh=mesh,
        in_specs=(P(None, ("outer", "inner")), P(("outer", "inner")), P()),
        out_specs=P(("outer", "inner"), None),
        check_vma=False,
    )
```

```python
import functools
import math

import jax
import jax.numpy as jnp
from jax import lax
from jax.experimental import pallas as pl
from jax.experimental.pallas import tpu as pltpu
from jax.sharding import PartitionSpec as P

MESH = pl.DeviceIdType.MESH
LANES = 128
DEPTH = 256
PACK = 16
GROUPS = [2, 6, 4, 4]
LEADS = [1, 1, 1, 1]
SETS = [[0, 0, 0, 0], [1, 1, 1, 1], [2, 2, 2, 2], [4, 3, 3, 3]]
WEIGHTS = [10, 20, 31, 60]
ROUTES = [[(0, 3), (0, 2), (0, 1), (0, 0), (1, 3), (1, 2), (1, 1), (1, 0), (2, 3), (2, 2), (2, 1), (2, 0), (3, 3), (3, 2), (3, 1), (3, 0)], [(0, 3), (0, 2), (0, 1), (0, 0), (2, 3), (2, 2), (2, 1), (2, 0), (1, 3), (1, 2), (1, 1), (1, 0), (3, 4), (3, 5), (3, 6), (3, 7)], [(0, 3), (0, 2), (0, 1), (0, 0), (1, 3), (1, 2), (1, 1), (1, 0), (3, 3), (3, 2), (3, 1), (3, 0), (2, 3), (2, 2), (2, 1), (2, 0)], [(0, 3), (0, 2), (0, 1), (0, 0), (1, 3), (1, 2), (1, 1), (1, 0), (3, 3), (3, 2), (3, 1), (3, 0), (2, 3), (2, 2), (2, 1), (2, 0)]]


def bit_parity(values):
    folded = jnp.bitwise_xor(values, jnp.right_shift(values, 16))
    folded = jnp.bitwise_xor(folded, jnp.right_shift(folded, 8))
    folded = jnp.bitwise_xor(folded, jnp.right_shift(folded, 4))
    folded = jnp.bitwise_xor(folded, jnp.right_shift(folded, 2))
    folded = jnp.bitwise_xor(folded, jnp.right_shift(folded, 1))
    return jnp.bitwise_and(folded, 1)


def hadamard(order_size):
    positions = lax.iota(jnp.int32, order_size)
    shared = jnp.bitwise_and(positions[:, None], positions[None, :])
    return jnp.where(bit_parity(shared) == 0, 1.0, -1.0).astype(jnp.float32)


def scatter_form(matrix_panel, row_signs, kept_rows):
    highest = lax.Precision.HIGHEST
    columns, local_rows = matrix_panel.shape
    outer_count = lax.axis_size("outer")
    inner_count = lax.axis_size("inner")
    device_count = outer_count * inner_count
    total_rows = local_rows * device_count
    me_outer = lax.axis_index("outer")
    me_inner = lax.axis_index("inner")
    signed = matrix_panel * row_signs.astype(jnp.float32)[None, :]
    leading = 128
    trailing = local_rows // leading
    blocks = signed.reshape(columns, leading, trailing)
    blocks = jnp.einsum("ap,jpq->jaq", hadamard(leading), blocks, precision=highest)
    blocks = jnp.einsum("bq,jaq->jab", hadamard(trailing), blocks, precision=highest)
    local_mix = blocks.reshape(columns, local_rows)
    low_bits = kept_rows % local_rows
    high_outer = kept_rows // (local_rows * inner_count)
    high_inner = kept_rows // local_rows % inner_count
    flips = bit_parity(jnp.bitwise_and(high_outer, me_outer)) + bit_parity(
        jnp.bitwise_and(high_inner, me_inner)
    )
    parity_sign = jnp.where(flips % 2 == 0, 1.0, -1.0).astype(jnp.float32)
    values = jnp.take(local_mix, low_bits, axis=1)
    summed = lax.psum_scatter(
        (values * parity_sign[None, :]).T, ("outer", "inner"), scatter_dimension=0, tiled=True
    )
    return summed * (1.0 / math.sqrt(total_rows))


def log2(size):
    return size.bit_length() - 1


def sign_of_bit(rows, bit):
    return (1 - 2 * jnp.bitwise_and(jnp.right_shift(rows, bit), 1)).astype(jnp.float32)


def bit_of(index, bit):
    return jnp.bitwise_and(jnp.right_shift(index, bit), 1)


def routes(far_count, side_count):
    if far_count == 4 and side_count == 4:
        return ROUTES
    return [[(far, side) for far in range(far_count) for side in reversed(range(side_count))] for _ in range(far_count)]


def ready_sets(far_count, side_count):
    if far_count == 4 and side_count == 4:
        return SETS
    return [[far] * side_count for far in range(far_count)]


def key_weights(side_bits, far_bits):
    if side_bits == 2 and far_bits == 2:
        return WEIGHTS
    return [1 << bit for bit in range(side_bits + far_bits)]


def kernel(
    outer_count, inner_count, scale,
    panel_hbm, signs_hbm, kept_hbm, out_ref,
    panel_ref, signs_ref, kept_ref, upper_ref, lower_ref, mix_ref, bits_ref, send_ref, recv_ref,
    load_sem, swap_send, swap_recv, send_sem, recv_sem, ready_sem,
):
    device_count = outer_count * inner_count
    chip_count = device_count // 2
    chip_bits = log2(chip_count)
    inner_bits = log2(inner_count)
    near_bits = min(1, inner_bits)
    far_bits = inner_bits - near_bits
    far_count = 1 << far_bits
    side_bits = chip_bits - far_bits
    side_count = 1 << side_bits
    columns, local_rows = panel_hbm.shape
    half = columns // 2
    mids = local_rows // DEPTH
    rows = 2 * mids * half
    me_outer = lax.axis_index("outer")
    me_inner = lax.axis_index("inner")
    me_core = bit_of(me_outer, 0)
    me_chip = jnp.right_shift(me_outer, 1) * inner_count + me_inner
    me_far = jnp.right_shift(me_inner, near_bits)
    me_side = jnp.right_shift(me_outer, 1) * (1 << near_bits) + jnp.bitwise_and(me_inner, (1 << near_bits) - 1)
    partner = (jnp.bitwise_xor(me_outer, 1), me_inner)

    own_rows = pl.ds(pl.multiple_of(me_core * half, half), half)
    other_rows = pl.ds(pl.multiple_of((1 - me_core) * half, half), half)
    loads = [
        pltpu.make_async_copy(source, target, load_sem.at[spot])
        for spot, (source, target) in enumerate(
            [
                (kept_hbm, kept_ref),
                (signs_hbm, signs_ref.at[me_core]),
                (panel_hbm.at[own_rows, :], panel_ref.at[me_core]),
            ]
        )
    ]

    for load in loads:
        load.start()

    weights = key_weights(side_bits, far_bits)
    sets = ready_sets(far_count, side_count)
    set_count = 1 + max(max(row) for row in sets)

    def key_of(far, side):
        bits = [side >> bit & 1 for bit in range(side_bits)] + [far >> bit & 1 for bit in range(far_bits)]
        return sum(weight * bit for weight, bit in zip(weights, bits))

    chips_by_key = sorted((key_of(far, side), far, side) for far in range(far_count) for side in range(side_count))
    me_key = 0
    for bit in range(side_bits):
        me_key = me_key + weights[bit] * bit_of(me_side, bit)
    for bit in range(far_bits):
        me_key = me_key + weights[side_bits + bit] * bit_of(me_far, bit)
    me_set = 0
    for far in range(far_count):
        for side in range(side_count):
            if sets[far][side]:
                me_set = jnp.where((me_far == far) & (me_side == side), sets[far][side], me_set)
    earlier = 0
    for key, _, _ in chips_by_key:
        earlier = earlier + jnp.where(key < me_key, 1, 0)
    pair, relay = set_count, set_count + 1

    def at(far, side, core):
        near = side & ((1 << near_bits) - 1)
        return ((side >> near_bits) * 2 + core, (far << near_bits) + near)

    def tell(semaphore, device):
        pl.semaphore_signal(semaphore, inc=1, device_id=device, device_id_type=MESH)

    barrier = pltpu.get_barrier_semaphore()

    @pl.when(me_core == 0)
    def _():
        tell(barrier, partner)

    for key, far, side in reversed(chips_by_key):
        @pl.when(me_key < key)
        def _(far=far, side=side):
            tell(barrier, at(far, side, 0))

    swaps = [
        pltpu.make_async_remote_copy(
            src_ref=source, dst_ref=target, send_sem=swap_send.at[spot], recv_sem=swap_recv.at[spot],
            device_id=partner, device_id_type=MESH,
        )
        for spot, (source, target) in enumerate(
            [(signs_hbm, signs_ref.at[me_core]), (panel_hbm.at[other_rows, :], panel_ref.at[me_core])]
        )
    ]

    @pl.when(me_core == 1)
    def _():
        pl.semaphore_wait(barrier, 1)
        tell(ready_sem.at[pair], partner)

    @pl.when(me_core == 0)
    def _():
        pl.semaphore_wait(ready_sem.at[pair], 1)

    for swap in swaps:
        swap.start()

    def settle():
        @pl.when(earlier > 0)
        def _():
            pl.semaphore_wait(barrier, 2 * earlier)

        tell(ready_sem.at[relay], partner)
        for key, far, side in chips_by_key:
            @pl.when(me_key > key)
            def _(far=far, side=side):
                for core in range(2):
                    tell(ready_sem.at[me_set], at(far, side, core))

    @pl.when((me_core == 0) & ((me_side == side_count - 1) | ((me_far == far_count - 1) & (me_side > 0))))
    def _():
        settle()

    core_bit = log2(local_rows) + inner_bits
    chip_at = [log2(local_rows) + bit for bit in range(inner_bits)]
    chip_at += [core_bit + 1 + bit for bit in range(chip_bits - inner_bits)]
    fold_bits = [core_bit] + [bit for bit in reversed(range(log2(DEPTH), log2(local_rows)))]

    loads[0].wait()

    def signs_of(tile, carry):
        first = jnp.right_shift(tile, inner_bits) * 2 * inner_count + jnp.bitwise_and(tile, inner_count - 1)
        kept = jnp.concatenate(
            [
                kept_ref[:, pl.ds(pl.multiple_of(block * LANES, LANES), LANES)]
                for block in (first, first + inner_count)
            ],
            axis=1,
        )
        width = 2 * LANES
        for spot, bit in enumerate(fold_bits):
            bits_ref[tile, spot:spot + 1, :] = sign_of_bit(kept, bit)
        plane = jnp.full((1, width), scale, jnp.float32)
        for bit, position in enumerate(chip_at):
            plane = plane * jnp.where(bit_of(me_chip, bit) == 1, sign_of_bit(kept, position), 1.0)
        bits_ref[tile, len(fold_bits):len(fold_bits) + 1, :] = plane
        position = lax.broadcasted_iota(jnp.int32, (PACK, width), 0)
        base = jnp.ones((PACK, width), jnp.float32)
        for bit in range(log2(PACK)):
            taken = jnp.bitwise_and(jnp.right_shift(position, bit), 1) == 1
            base = base * jnp.where(taken, sign_of_bit(kept, bit), 1.0)
        blocks = [base.astype(jnp.bfloat16)]
        for bit in range(log2(PACK), log2(DEPTH)):
            flip = jnp.broadcast_to(sign_of_bit(kept, bit), (PACK, width)).astype(jnp.bfloat16)
            blocks = blocks + [block * flip for block in blocks]
        for top, block in enumerate(blocks):
            mix_ref[tile, top * PACK:(top + 1) * PACK, :] = block
        return carry

    lax.fori_loop(0, chip_count, signs_of, 0)

    @pl.when((me_core == 0) & (me_side > 0) & (me_side < side_count - 1) & jnp.logical_not((me_far == far_count - 1)))
    def _():
        settle()


    def split(core):
        for mid in range(mids):
            lanes = slice(mid * DEPTH, (mid + 1) * DEPTH)
            block = panel_ref[core, :, lanes] * signs_ref[core, :, lanes].astype(jnp.float32)
            upper = block.astype(jnp.bfloat16)
            lower = (block - upper.astype(jnp.float32)).astype(jnp.bfloat16)
            upper_ref[core, mid * half:(mid + 1) * half, :] = upper
            lower_ref[core, mid * half:(mid + 1) * half, :] = lower

    for load in loads[1:]:
        load.wait()
    split(me_core)
    for swap in swaps:
        swap.wait_recv()
    split(1 - me_core)

    def parts_of(tiles):
        upper = upper_ref[...].reshape(rows, DEPTH)
        lower = lower_ref[...].reshape(rows, DEPTH)
        parts = []
        for tile in tiles:
            mix = mix_ref[tile]
            part = jnp.dot(upper, mix, preferred_element_type=jnp.float32)
            parts.append(part + jnp.dot(lower, mix, preferred_element_type=jnp.float32))
        for spot in range(len(fold_bits)):
            size = rows >> (spot + 1)
            parts = [
                part[:size] + part[size:] * bits_ref[tile, spot:spot + 1, :] for part, tile in zip(parts, tiles)
            ]
        plane = len(fold_bits)
        return [part * bits_ref[tile, plane:plane + 1, :] for part, tile in zip(parts, tiles)]

    mine = me_chip * 2 + me_core

    def own_at(slot):
        @pl.when(me_core == 0)
        def _():
            recv_ref[mine] = send_ref[slot]

        @pl.when(me_core == 1)
        def _():
            recv_ref[mine] = send_ref[slot + 1]

    def start(slot, chip, core):
        pltpu.make_async_remote_copy(
            src_ref=send_ref.at[slot + core],
            dst_ref=recv_ref.at[mine],
            send_sem=send_sem,
            recv_sem=recv_sem,
            device_id=(jnp.right_shift(chip, inner_bits) * 2 + core, jnp.bitwise_and(chip, inner_count - 1)),
            device_id_type=MESH,
        ).start()

    def start_both(slot, chip, maybe_own):
        cores = (0, 1) if slot == 0 else (1, 0)
        if not maybe_own:
            for core in cores:
                start(slot, chip, core)
            return
        own = chip == me_chip
        for core in cores:
            @pl.when(jnp.logical_not(own & (me_core == core)))
            def _(core=core):
                start(slot, chip, core)

        @pl.when(own)
        def _():
            own_at(slot)

    def keep(slot, part):
        send_ref[slot] = part[:, :LANES]
        send_ref[slot + 1] = part[:, LANES:]

    plans = routes(far_count, side_count)

    def by_row(values):
        picked = values[0]
        for row, value in enumerate(values[1:], 1):
            if value != values[0]:
                picked = jnp.where(me_far == row, value, picked)
        return picked

    def waited(chosen):
        total = 0
        for key, far, side in chips_by_key:
            if sets[far][side] == chosen:
                total = total + jnp.where(key > me_key, 1, 0)
        return total

    wanted = [waited(chosen) for chosen in range(set_count)]
    opened = [set() for _ in range(far_count)]
    place = 0
    for size in GROUPS if chip_count == sum(GROUPS) else [1] * chip_count:
        chips = []
        for spot in range(place, place + size):
            far = by_row([plan[spot][0] for plan in plans])
            swapped = by_row([plan[spot][1] % side_count for plan in plans])
            for row, plan in enumerate(plans):
                value = None
                if LEADS[row % len(LEADS)] and plan[spot][0] == 0:
                    start_spot = min(index for index, one in enumerate(plan) if one[0] == 0)
                    lead = plan[start_spot][1]
                    value = me_side if spot == start_spot else jnp.where(swapped == me_side, lead, swapped)
                elif plan[spot][1] >= side_count:
                    value = jnp.bitwise_xor(me_side, plan[spot][1] - side_count)
                if value is not None:
                    swapped = jnp.where(me_far == row, value, swapped)
            side = jnp.bitwise_xor(me_side, swapped)
            upper = jnp.right_shift(side, near_bits) * inner_count
            chips.append(upper + far * (1 << near_bits) + jnp.bitwise_and(side, (1 << near_bits) - 1))
        for spot, part in enumerate(parts_of(chips), place):
            keep(spot * 2, part)
        if place == 0:
            @pl.when((me_core == 0) & (me_side == 0))
            def _():
                settle()

            @pl.when(me_core == 1)
            def _():
                pl.semaphore_wait(ready_sem.at[relay], 1)

        for spot, chip in enumerate(chips, place):
            fresh = {}
            for row, plan in enumerate(plans):
                far, side = plan[spot]
                reached = [sets[far][side - side_count]] if side >= side_count else sets[far]
                for chosen in sorted(set(reached) - opened[row]):
                    opened[row].add(chosen)
                    fresh.setdefault(chosen, []).append(row)
            for chosen, opening in fresh.items():
                here = me_far == opening[0]
                for row in opening[1:]:
                    here = here | (me_far == row)

                @pl.when(here & (wanted[chosen] > 0))
                def _(chosen=chosen):
                    pl.semaphore_wait(ready_sem.at[chosen], wanted[chosen])

            own = any(
                plan[spot][0] == row and (plan[spot][1] % side_count == 0 or plan[spot][1] >= side_count or row == 0)
                for row, plan in enumerate(plans)
            )
            start_both(spot * 2, chip, own)
        place += size
    for swap in swaps:
        swap.wait_send()
    everything = pltpu.make_async_remote_copy(
        src_ref=send_ref.at[pl.ds(0, device_count - 1)],
        dst_ref=recv_ref.at[pl.ds(0, device_count - 1)],
        send_sem=send_sem,
        recv_sem=recv_sem,
        device_id=partner,
        device_id_type=MESH,
    )
    everything.wait_send()
    everything.wait_recv()
    for core in range(2):
        terms = [recv_ref[chip * 2 + core] for chip in range(chip_count)]
        while len(terms) > 1:
            terms = [one + other for one, other in zip(terms[::2], terms[1::2])]
        out_ref[core * half:(core + 1) * half, :] = terms[0]


def solution(mesh):
    outer_count, inner_count = mesh.shape["outer"], mesh.shape["inner"]
    device_count = outer_count * inner_count

    def local(matrix_panel, row_signs, kept_rows):
        columns, local_rows = matrix_panel.shape
        kept_count = kept_rows.shape[0]
        half = columns // 2
        powers = all(size & (size - 1) == 0 for size in (outer_count, inner_count, local_rows))
        fits = (
            powers
            and outer_count % 2 == 0
            and device_count >= 4
            and columns % (2 * PACK) == 0
            and kept_count == device_count * LANES
            and local_rows % (2 * DEPTH) == 0
        )
        if not fits:
            return scatter_form(matrix_panel, row_signs, kept_rows)
        mids = local_rows // DEPTH
        chips = device_count // 2
        arrived = pl.pallas_call(
            functools.partial(kernel, outer_count, inner_count, 1.0 / math.sqrt(local_rows * device_count)),
            out_shape=pltpu.VMEM((columns, LANES), jnp.float32),
            in_specs=[pl.BlockSpec(memory_space=pl.ANY)] * 3,
            out_specs=pl.BlockSpec(memory_space=pltpu.VMEM),
            scratch_shapes=[
                pltpu.VMEM((2, half, local_rows), jnp.float32),
                pltpu.VMEM((2, 1, local_rows), jnp.int32),
                pltpu.VMEM((1, kept_count), jnp.int32),
                pltpu.VMEM((2, mids * half, DEPTH), jnp.bfloat16),
                pltpu.VMEM((2, mids * half, DEPTH), jnp.bfloat16),
                pltpu.VMEM((chips, DEPTH, 2 * LANES), jnp.bfloat16),
                pltpu.VMEM((chips, 8, 2 * LANES), jnp.float32),
                pltpu.VMEM((device_count, half, LANES), jnp.float32),
                pltpu.VMEM((device_count, half, LANES), jnp.float32),
                pltpu.SemaphoreType.DMA((3,)),
                pltpu.SemaphoreType.DMA((2,)),
                pltpu.SemaphoreType.DMA((2,)),
                pltpu.SemaphoreType.DMA(()),
                pltpu.SemaphoreType.DMA(()),
                pltpu.SemaphoreType.REGULAR((max(inner_count // 2 + 2, 8),)),
            ],
            compiler_params=pltpu.CompilerParams(collective_id=0, has_side_effects=True),
        )(matrix_panel, row_signs.reshape(1, local_rows), kept_rows.reshape(1, kept_count))
        return arrived.T

    return jax.shard_map(
        local,
        mesh=mesh,
        in_specs=(P(None, ("outer", "inner")), P(("outer", "inner")), P()),
        out_specs=P(("outer", "inner"), None),
        check_vma=False,
    )
```

```python
import functools
import math

import jax
import jax.numpy as jnp
from jax import lax
from jax.experimental import pallas as pl
from jax.experimental.pallas import tpu as pltpu
from jax.sharding import PartitionSpec as P

MESH = pl.DeviceIdType.MESH
LANES = 128
DEPTH = 256
PACK = 16
GROUPS = [2, 6, 6, 2]
LEADS = [1, 1, 1, 1]
SETS = [[0, 0, 0, 0], [1, 1, 1, 1], [2, 2, 2, 2], [4, 3, 3, 3]]
WEIGHTS = [10, 20, 31, 60]
ROUTES = [[(0, 3), (0, 2), (0, 1), (0, 0), (1, 3), (1, 2), (1, 1), (1, 0), (2, 3), (2, 2), (2, 1), (2, 0), (3, 3), (3, 2), (3, 1), (3, 0)], [(0, 3), (0, 2), (0, 1), (0, 0), (2, 3), (2, 2), (2, 1), (2, 0), (1, 3), (1, 2), (1, 1), (1, 0), (3, 4), (3, 5), (3, 6), (3, 7)], [(0, 3), (0, 2), (0, 1), (0, 0), (1, 3), (1, 2), (1, 1), (1, 0), (3, 3), (3, 2), (3, 1), (3, 0), (2, 3), (2, 2), (2, 1), (2, 0)], [(0, 3), (0, 2), (0, 1), (0, 0), (1, 3), (1, 2), (1, 1), (1, 0), (3, 3), (3, 2), (3, 1), (3, 0), (2, 3), (2, 2), (2, 1), (2, 0)]]


def bit_parity(values):
    folded = jnp.bitwise_xor(values, jnp.right_shift(values, 16))
    folded = jnp.bitwise_xor(folded, jnp.right_shift(folded, 8))
    folded = jnp.bitwise_xor(folded, jnp.right_shift(folded, 4))
    folded = jnp.bitwise_xor(folded, jnp.right_shift(folded, 2))
    folded = jnp.bitwise_xor(folded, jnp.right_shift(folded, 1))
    return jnp.bitwise_and(folded, 1)


def hadamard(order_size):
    positions = lax.iota(jnp.int32, order_size)
    shared = jnp.bitwise_and(positions[:, None], positions[None, :])
    return jnp.where(bit_parity(shared) == 0, 1.0, -1.0).astype(jnp.float32)


def scatter_form(matrix_panel, row_signs, kept_rows):
    highest = lax.Precision.HIGHEST
    columns, local_rows = matrix_panel.shape
    outer_count = lax.axis_size("outer")
    inner_count = lax.axis_size("inner")
    device_count = outer_count * inner_count
    total_rows = local_rows * device_count
    me_outer = lax.axis_index("outer")
    me_inner = lax.axis_index("inner")
    signed = matrix_panel * row_signs.astype(jnp.float32)[None, :]
    leading = 128
    trailing = local_rows // leading
    blocks = signed.reshape(columns, leading, trailing)
    blocks = jnp.einsum("ap,jpq->jaq", hadamard(leading), blocks, precision=highest)
    blocks = jnp.einsum("bq,jaq->jab", hadamard(trailing), blocks, precision=highest)
    local_mix = blocks.reshape(columns, local_rows)
    low_bits = kept_rows % local_rows
    high_outer = kept_rows // (local_rows * inner_count)
    high_inner = kept_rows // local_rows % inner_count
    flips = bit_parity(jnp.bitwise_and(high_outer, me_outer)) + bit_parity(
        jnp.bitwise_and(high_inner, me_inner)
    )
    parity_sign = jnp.where(flips % 2 == 0, 1.0, -1.0).astype(jnp.float32)
    values = jnp.take(local_mix, low_bits, axis=1)
    summed = lax.psum_scatter(
        (values * parity_sign[None, :]).T, ("outer", "inner"), scatter_dimension=0, tiled=True
    )
    return summed * (1.0 / math.sqrt(total_rows))


def log2(size):
    return size.bit_length() - 1


def sign_of_bit(rows, bit):
    return (1 - 2 * jnp.bitwise_and(jnp.right_shift(rows, bit), 1)).astype(jnp.float32)


def bit_of(index, bit):
    return jnp.bitwise_and(jnp.right_shift(index, bit), 1)


def routes(far_count, side_count):
    if far_count == 4 and side_count == 4:
        return ROUTES
    return [[(far, side) for far in range(far_count) for side in reversed(range(side_count))] for _ in range(far_count)]


def ready_sets(far_count, side_count):
    if far_count == 4 and side_count == 4:
        return SETS
    return [[far] * side_count for far in range(far_count)]


def key_weights(side_bits, far_bits):
    if side_bits == 2 and far_bits == 2:
        return WEIGHTS
    return [1 << bit for bit in range(side_bits + far_bits)]


def kernel(
    outer_count, inner_count, scale,
    panel_hbm, signs_hbm, kept_hbm, out_ref,
    panel_ref, signs_ref, kept_ref, upper_ref, lower_ref, mix_ref, bits_ref, send_ref, recv_ref,
    load_sem, swap_send, swap_recv, send_sem, recv_sem, ready_sem,
):
    device_count = outer_count * inner_count
    chip_count = device_count // 2
    chip_bits = log2(chip_count)
    inner_bits = log2(inner_count)
    near_bits = min(1, inner_bits)
    far_bits = inner_bits - near_bits
    far_count = 1 << far_bits
    side_bits = chip_bits - far_bits
    side_count = 1 << side_bits
    columns, local_rows = panel_hbm.shape
    half = columns // 2
    mids = local_rows // DEPTH
    rows = 2 * mids * half
    me_outer = lax.axis_index("outer")
    me_inner = lax.axis_index("inner")
    me_core = bit_of(me_outer, 0)
    me_chip = jnp.right_shift(me_outer, 1) * inner_count + me_inner
    me_far = jnp.right_shift(me_inner, near_bits)
    me_side = jnp.right_shift(me_outer, 1) * (1 << near_bits) + jnp.bitwise_and(me_inner, (1 << near_bits) - 1)
    partner = (jnp.bitwise_xor(me_outer, 1), me_inner)

    own_rows = pl.ds(pl.multiple_of(me_core * half, half), half)
    other_rows = pl.ds(pl.multiple_of((1 - me_core) * half, half), half)
    loads = [
        pltpu.make_async_copy(source, target, load_sem.at[spot])
        for spot, (source, target) in enumerate(
            [
                (kept_hbm, kept_ref),
                (signs_hbm, signs_ref.at[me_core]),
                (panel_hbm.at[own_rows, :], panel_ref.at[me_core]),
            ]
        )
    ]

    for load in loads:
        load.start()

    weights = key_weights(side_bits, far_bits)
    sets = ready_sets(far_count, side_count)
    set_count = 1 + max(max(row) for row in sets)

    def key_of(far, side):
        bits = [side >> bit & 1 for bit in range(side_bits)] + [far >> bit & 1 for bit in range(far_bits)]
        return sum(weight * bit for weight, bit in zip(weights, bits))

    chips_by_key = sorted((key_of(far, side), far, side) for far in range(far_count) for side in range(side_count))
    me_key = 0
    for bit in range(side_bits):
        me_key = me_key + weights[bit] * bit_of(me_side, bit)
    for bit in range(far_bits):
        me_key = me_key + weights[side_bits + bit] * bit_of(me_far, bit)
    me_set = 0
    for far in range(far_count):
        for side in range(side_count):
            if sets[far][side]:
                me_set = jnp.where((me_far == far) & (me_side == side), sets[far][side], me_set)
    earlier = 0
    for key, _, _ in chips_by_key:
        earlier = earlier + jnp.where(key < me_key, 1, 0)
    pair, relay = set_count, set_count + 1

    def at(far, side, core):
        near = side & ((1 << near_bits) - 1)
        return ((side >> near_bits) * 2 + core, (far << near_bits) + near)

    def tell(semaphore, device):
        pl.semaphore_signal(semaphore, inc=1, device_id=device, device_id_type=MESH)

    barrier = pltpu.get_barrier_semaphore()

    @pl.when(me_core == 0)
    def _():
        tell(barrier, partner)

    for key, far, side in reversed(chips_by_key):
        @pl.when(me_key < key)
        def _(far=far, side=side):
            tell(barrier, at(far, side, 0))

    swaps = [
        pltpu.make_async_remote_copy(
            src_ref=source, dst_ref=target, send_sem=swap_send.at[spot], recv_sem=swap_recv.at[spot],
            device_id=partner, device_id_type=MESH,
        )
        for spot, (source, target) in enumerate(
            [(signs_hbm, signs_ref.at[me_core]), (panel_hbm.at[other_rows, :], panel_ref.at[me_core])]
        )
    ]

    @pl.when(me_core == 1)
    def _():
        pl.semaphore_wait(barrier, 1)
        tell(ready_sem.at[pair], partner)

    @pl.when(me_core == 0)
    def _():
        pl.semaphore_wait(ready_sem.at[pair], 1)

    for swap in swaps:
        swap.start()

    def settle():
        @pl.when(earlier > 0)
        def _():
            pl.semaphore_wait(barrier, 2 * earlier)

        tell(ready_sem.at[relay], partner)
        for key, far, side in chips_by_key:
            @pl.when(me_key > key)
            def _(far=far, side=side):
                for core in range(2):
                    tell(ready_sem.at[me_set], at(far, side, core))

    @pl.when((me_core == 0) & ((me_side == side_count - 1) | ((me_far == far_count - 1) & (me_side > 0))))
    def _():
        settle()

    core_bit = log2(local_rows) + inner_bits
    chip_at = [log2(local_rows) + bit for bit in range(inner_bits)]
    chip_at += [core_bit + 1 + bit for bit in range(chip_bits - inner_bits)]
    fold_bits = [core_bit] + [bit for bit in reversed(range(log2(DEPTH), log2(local_rows)))]

    loads[0].wait()

    def signs_of(tile, carry):
        first = jnp.right_shift(tile, inner_bits) * 2 * inner_count + jnp.bitwise_and(tile, inner_count - 1)
        kept = jnp.concatenate(
            [
                kept_ref[:, pl.ds(pl.multiple_of(block * LANES, LANES), LANES)]
                for block in (first, first + inner_count)
            ],
            axis=1,
        )
        width = 2 * LANES
        for spot, bit in enumerate(fold_bits):
            bits_ref[tile, spot:spot + 1, :] = sign_of_bit(kept, bit)
        plane = jnp.full((1, width), scale, jnp.float32)
        for bit, position in enumerate(chip_at):
            plane = plane * jnp.where(bit_of(me_chip, bit) == 1, sign_of_bit(kept, position), 1.0)
        bits_ref[tile, len(fold_bits):len(fold_bits) + 1, :] = plane
        position = lax.broadcasted_iota(jnp.int32, (PACK, width), 0)
        base = jnp.ones((PACK, width), jnp.float32)
        for bit in range(log2(PACK)):
            taken = jnp.bitwise_and(jnp.right_shift(position, bit), 1) == 1
            base = base * jnp.where(taken, sign_of_bit(kept, bit), 1.0)
        blocks = [base.astype(jnp.bfloat16)]
        for bit in range(log2(PACK), log2(DEPTH)):
            flip = jnp.broadcast_to(sign_of_bit(kept, bit), (PACK, width)).astype(jnp.bfloat16)
            blocks = blocks + [block * flip for block in blocks]
        for top, block in enumerate(blocks):
            mix_ref[tile, top * PACK:(top + 1) * PACK, :] = block
        return carry

    lax.fori_loop(0, chip_count, signs_of, 0)

    @pl.when((me_core == 0) & (me_side > 0) & (me_side < side_count - 1) & jnp.logical_not((me_far == far_count - 1)))
    def _():
        settle()


    def split(core):
        for mid in range(mids):
            lanes = slice(mid * DEPTH, (mid + 1) * DEPTH)
            block = panel_ref[core, :, lanes] * signs_ref[core, :, lanes].astype(jnp.float32)
            upper = block.astype(jnp.bfloat16)
            lower = (block - upper.astype(jnp.float32)).astype(jnp.bfloat16)
            upper_ref[core, mid * half:(mid + 1) * half, :] = upper
            lower_ref[core, mid * half:(mid + 1) * half, :] = lower

    for load in loads[1:]:
        load.wait()
    split(me_core)
    for swap in swaps:
        swap.wait_recv()
    split(1 - me_core)

    def parts_of(tiles):
        upper = upper_ref[...].reshape(rows, DEPTH)
        lower = lower_ref[...].reshape(rows, DEPTH)
        parts = []
        for tile in tiles:
            mix = mix_ref[tile]
            part = jnp.dot(upper, mix, preferred_element_type=jnp.float32)
            parts.append(part + jnp.dot(lower, mix, preferred_element_type=jnp.float32))
        for spot in range(len(fold_bits)):
            size = rows >> (spot + 1)
            parts = [
                part[:size] + part[size:] * bits_ref[tile, spot:spot + 1, :] for part, tile in zip(parts, tiles)
            ]
        plane = len(fold_bits)
        return [part * bits_ref[tile, plane:plane + 1, :] for part, tile in zip(parts, tiles)]

    mine = me_chip * 2 + me_core

    def own_at(slot):
        @pl.when(me_core == 0)
        def _():
            recv_ref[mine] = send_ref[slot]

        @pl.when(me_core == 1)
        def _():
            recv_ref[mine] = send_ref[slot + 1]

    def start(slot, chip, core):
        pltpu.make_async_remote_copy(
            src_ref=send_ref.at[slot + core],
            dst_ref=recv_ref.at[mine],
            send_sem=send_sem,
            recv_sem=recv_sem,
            device_id=(jnp.right_shift(chip, inner_bits) * 2 + core, jnp.bitwise_and(chip, inner_count - 1)),
            device_id_type=MESH,
        ).start()

    def start_both(slot, chip, maybe_own):
        cores = (0, 1) if slot == 0 else (1, 0)
        if not maybe_own:
            for core in cores:
                start(slot, chip, core)
            return
        own = chip == me_chip
        for core in cores:
            @pl.when(jnp.logical_not(own & (me_core == core)))
            def _(core=core):
                start(slot, chip, core)

        @pl.when(own)
        def _():
            own_at(slot)

    def keep(slot, part):
        send_ref[slot] = part[:, :LANES]
        send_ref[slot + 1] = part[:, LANES:]

    plans = routes(far_count, side_count)

    def by_row(values):
        picked = values[0]
        for row, value in enumerate(values[1:], 1):
            if value != values[0]:
                picked = jnp.where(me_far == row, value, picked)
        return picked

    def waited(chosen):
        total = 0
        for key, far, side in chips_by_key:
            if sets[far][side] == chosen:
                total = total + jnp.where(key > me_key, 1, 0)
        return total

    wanted = [waited(chosen) for chosen in range(set_count)]
    opened = [set() for _ in range(far_count)]
    place = 0
    for size in GROUPS if chip_count == sum(GROUPS) else [1] * chip_count:
        chips = []
        for spot in range(place, place + size):
            far = by_row([plan[spot][0] for plan in plans])
            swapped = by_row([plan[spot][1] % side_count for plan in plans])
            for row, plan in enumerate(plans):
                value = None
                if LEADS[row % len(LEADS)] and plan[spot][0] == 0:
                    start_spot = min(index for index, one in enumerate(plan) if one[0] == 0)
                    lead = plan[start_spot][1]
                    value = me_side if spot == start_spot else jnp.where(swapped == me_side, lead, swapped)
                elif plan[spot][1] >= side_count:
                    value = jnp.bitwise_xor(me_side, plan[spot][1] - side_count)
                if value is not None:
                    swapped = jnp.where(me_far == row, value, swapped)
            side = jnp.bitwise_xor(me_side, swapped)
            upper = jnp.right_shift(side, near_bits) * inner_count
            chips.append(upper + far * (1 << near_bits) + jnp.bitwise_and(side, (1 << near_bits) - 1))
        for spot, part in enumerate(parts_of(chips), place):
            keep(spot * 2, part)
        if place == 0:
            @pl.when((me_core == 0) & (me_side == 0))
            def _():
                settle()

            @pl.when(me_core == 1)
            def _():
                pl.semaphore_wait(ready_sem.at[relay], 1)

        for spot, chip in enumerate(chips, place):
            fresh = {}
            for row, plan in enumerate(plans):
                far, side = plan[spot]
                reached = [sets[far][side - side_count]] if side >= side_count else sets[far]
                for chosen in sorted(set(reached) - opened[row]):
                    opened[row].add(chosen)
                    fresh.setdefault(chosen, []).append(row)
            for chosen, opening in fresh.items():
                here = me_far == opening[0]
                for row in opening[1:]:
                    here = here | (me_far == row)

                @pl.when(here & (wanted[chosen] > 0))
                def _(chosen=chosen):
                    pl.semaphore_wait(ready_sem.at[chosen], wanted[chosen])

            own = any(
                plan[spot][0] == row and (plan[spot][1] % side_count == 0 or plan[spot][1] >= side_count or row == 0)
                for row, plan in enumerate(plans)
            )
            start_both(spot * 2, chip, own)
        place += size
    for swap in swaps:
        swap.wait_send()
    everything = pltpu.make_async_remote_copy(
        src_ref=send_ref.at[pl.ds(0, device_count - 1)],
        dst_ref=recv_ref.at[pl.ds(0, device_count - 1)],
        send_sem=send_sem,
        recv_sem=recv_sem,
        device_id=partner,
        device_id_type=MESH,
    )
    everything.wait_send()
    everything.wait_recv()
    for core in range(2):
        terms = [recv_ref[chip * 2 + core] for chip in range(chip_count)]
        while len(terms) > 1:
            terms = [one + other for one, other in zip(terms[::2], terms[1::2])]
        out_ref[core * half:(core + 1) * half, :] = terms[0]


def solution(mesh):
    outer_count, inner_count = mesh.shape["outer"], mesh.shape["inner"]
    device_count = outer_count * inner_count

    def local(matrix_panel, row_signs, kept_rows):
        columns, local_rows = matrix_panel.shape
        kept_count = kept_rows.shape[0]
        half = columns // 2
        powers = all(size & (size - 1) == 0 for size in (outer_count, inner_count, local_rows))
        fits = (
            powers
            and outer_count % 2 == 0
            and device_count >= 4
            and columns % (2 * PACK) == 0
            and kept_count == device_count * LANES
            and local_rows % (2 * DEPTH) == 0
        )
        if not fits:
            return scatter_form(matrix_panel, row_signs, kept_rows)
        mids = local_rows // DEPTH
        chips = device_count // 2
        arrived = pl.pallas_call(
            functools.partial(kernel, outer_count, inner_count, 1.0 / math.sqrt(local_rows * device_count)),
            out_shape=pltpu.VMEM((columns, LANES), jnp.float32),
            in_specs=[pl.BlockSpec(memory_space=pl.ANY)] * 3,
            out_specs=pl.BlockSpec(memory_space=pltpu.VMEM),
            scratch_shapes=[
                pltpu.VMEM((2, half, local_rows), jnp.float32),
                pltpu.VMEM((2, 1, local_rows), jnp.int32),
                pltpu.VMEM((1, kept_count), jnp.int32),
                pltpu.VMEM((2, mids * half, DEPTH), jnp.bfloat16),
                pltpu.VMEM((2, mids * half, DEPTH), jnp.bfloat16),
                pltpu.VMEM((chips, DEPTH, 2 * LANES), jnp.bfloat16),
                pltpu.VMEM((chips, 8, 2 * LANES), jnp.float32),
                pltpu.VMEM((device_count, half, LANES), jnp.float32),
                pltpu.VMEM((device_count, half, LANES), jnp.float32),
                pltpu.SemaphoreType.DMA((3,)),
                pltpu.SemaphoreType.DMA((2,)),
                pltpu.SemaphoreType.DMA((2,)),
                pltpu.SemaphoreType.DMA(()),
                pltpu.SemaphoreType.DMA(()),
                pltpu.SemaphoreType.REGULAR((max(inner_count // 2 + 2, 7),)),
            ],
            compiler_params=pltpu.CompilerParams(collective_id=0, has_side_effects=True),
        )(matrix_panel, row_signs.reshape(1, local_rows), kept_rows.reshape(1, kept_count))
        return arrived.T

    return jax.shard_map(
        local,
        mesh=mesh,
        in_specs=(P(None, ("outer", "inner")), P(("outer", "inner")), P()),
        out_specs=P(("outer", "inner"), None),
        check_vma=False,
    )
```

```python
import functools
import math

import jax
import jax.numpy as jnp
from jax import lax
from jax.experimental import pallas as pl
from jax.experimental.pallas import tpu as pltpu
from jax.sharding import PartitionSpec as P

MESH = pl.DeviceIdType.MESH
LANES = 128
DEPTH = 256
PACK = 16
GROUPS = [2, 6, 4, 4]
LEADS = [1, 1, 1, 1]
SETS = [[0, 0, 0, 0], [1, 1, 1, 1], [2, 2, 2, 2], [4, 3, 3, 3]]
WEIGHTS = [10, 20, 31, 60]
ROUTES = [[(0, 3), (0, 2), (0, 1), (0, 0), (1, 3), (1, 2), (1, 1), (1, 0), (2, 3), (2, 2), (2, 1), (2, 0), (3, 3), (3, 2), (3, 1), (3, 0)], [(0, 3), (0, 2), (0, 1), (0, 0), (2, 3), (2, 2), (2, 1), (2, 0), (1, 3), (1, 2), (1, 1), (1, 0), (3, 4), (3, 6), (3, 5), (3, 7)], [(0, 3), (0, 2), (0, 1), (0, 0), (1, 3), (1, 2), (1, 1), (1, 0), (3, 3), (3, 2), (3, 1), (3, 0), (2, 3), (2, 2), (2, 1), (2, 0)], [(0, 3), (0, 2), (0, 1), (0, 0), (1, 3), (1, 2), (1, 1), (1, 0), (3, 3), (3, 2), (3, 1), (3, 0), (2, 3), (2, 2), (2, 1), (2, 0)]]


def bit_parity(values):
    folded = jnp.bitwise_xor(values, jnp.right_shift(values, 16))
    folded = jnp.bitwise_xor(folded, jnp.right_shift(folded, 8))
    folded = jnp.bitwise_xor(folded, jnp.right_shift(folded, 4))
    folded = jnp.bitwise_xor(folded, jnp.right_shift(folded, 2))
    folded = jnp.bitwise_xor(folded, jnp.right_shift(folded, 1))
    return jnp.bitwise_and(folded, 1)


def hadamard(order_size):
    positions = lax.iota(jnp.int32, order_size)
    shared = jnp.bitwise_and(positions[:, None], positions[None, :])
    return jnp.where(bit_parity(shared) == 0, 1.0, -1.0).astype(jnp.float32)


def scatter_form(matrix_panel, row_signs, kept_rows):
    highest = lax.Precision.HIGHEST
    columns, local_rows = matrix_panel.shape
    outer_count = lax.axis_size("outer")
    inner_count = lax.axis_size("inner")
    device_count = outer_count * inner_count
    total_rows = local_rows * device_count
    me_outer = lax.axis_index("outer")
    me_inner = lax.axis_index("inner")
    signed = matrix_panel * row_signs.astype(jnp.float32)[None, :]
    leading = 128
    trailing = local_rows // leading
    blocks = signed.reshape(columns, leading, trailing)
    blocks = jnp.einsum("ap,jpq->jaq", hadamard(leading), blocks, precision=highest)
    blocks = jnp.einsum("bq,jaq->jab", hadamard(trailing), blocks, precision=highest)
    local_mix = blocks.reshape(columns, local_rows)
    low_bits = kept_rows % local_rows
    high_outer = kept_rows // (local_rows * inner_count)
    high_inner = kept_rows // local_rows % inner_count
    flips = bit_parity(jnp.bitwise_and(high_outer, me_outer)) + bit_parity(
        jnp.bitwise_and(high_inner, me_inner)
    )
    parity_sign = jnp.where(flips % 2 == 0, 1.0, -1.0).astype(jnp.float32)
    values = jnp.take(local_mix, low_bits, axis=1)
    summed = lax.psum_scatter(
        (values * parity_sign[None, :]).T, ("outer", "inner"), scatter_dimension=0, tiled=True
    )
    return summed * (1.0 / math.sqrt(total_rows))


def log2(size):
    return size.bit_length() - 1


def sign_of_bit(rows, bit):
    return (1 - 2 * jnp.bitwise_and(jnp.right_shift(rows, bit), 1)).astype(jnp.float32)


def bit_of(index, bit):
    return jnp.bitwise_and(jnp.right_shift(index, bit), 1)


def routes(far_count, side_count):
    if far_count == 4 and side_count == 4:
        return ROUTES
    return [[(far, side) for far in range(far_count) for side in reversed(range(side_count))] for _ in range(far_count)]


def ready_sets(far_count, side_count):
    if far_count == 4 and side_count == 4:
        return SETS
    return [[far] * side_count for far in range(far_count)]


def key_weights(side_bits, far_bits):
    if side_bits == 2 and far_bits == 2:
        return WEIGHTS
    return [1 << bit for bit in range(side_bits + far_bits)]


def kernel(
    outer_count, inner_count, scale,
    panel_hbm, signs_hbm, kept_hbm, out_ref,
    panel_ref, signs_ref, kept_ref, upper_ref, lower_ref, mix_ref, bits_ref, send_ref, recv_ref,
    load_sem, swap_send, swap_recv, send_sem, recv_sem, ready_sem,
):
    device_count = outer_count * inner_count
    chip_count = device_count // 2
    chip_bits = log2(chip_count)
    inner_bits = log2(inner_count)
    near_bits = min(1, inner_bits)
    far_bits = inner_bits - near_bits
    far_count = 1 << far_bits
    side_bits = chip_bits - far_bits
    side_count = 1 << side_bits
    columns, local_rows = panel_hbm.shape
    half = columns // 2
    mids = local_rows // DEPTH
    rows = 2 * mids * half
    me_outer = lax.axis_index("outer")
    me_inner = lax.axis_index("inner")
    me_core = bit_of(me_outer, 0)
    me_chip = jnp.right_shift(me_outer, 1) * inner_count + me_inner
    me_far = jnp.right_shift(me_inner, near_bits)
    me_side = jnp.right_shift(me_outer, 1) * (1 << near_bits) + jnp.bitwise_and(me_inner, (1 << near_bits) - 1)
    partner = (jnp.bitwise_xor(me_outer, 1), me_inner)

    own_rows = pl.ds(pl.multiple_of(me_core * half, half), half)
    other_rows = pl.ds(pl.multiple_of((1 - me_core) * half, half), half)
    loads = [
        pltpu.make_async_copy(source, target, load_sem.at[spot])
        for spot, (source, target) in enumerate(
            [
                (kept_hbm, kept_ref),
                (signs_hbm, signs_ref.at[me_core]),
                (panel_hbm.at[own_rows, :], panel_ref.at[me_core]),
            ]
        )
    ]

    weights = key_weights(side_bits, far_bits)
    sets = ready_sets(far_count, side_count)
    set_count = 1 + max(max(row) for row in sets)

    def key_of(far, side):
        bits = [side >> bit & 1 for bit in range(side_bits)] + [far >> bit & 1 for bit in range(far_bits)]
        return sum(weight * bit for weight, bit in zip(weights, bits))

    chips_by_key = sorted((key_of(far, side), far, side) for far in range(far_count) for side in range(side_count))
    me_key = 0
    for bit in range(side_bits):
        me_key = me_key + weights[bit] * bit_of(me_side, bit)
    for bit in range(far_bits):
        me_key = me_key + weights[side_bits + bit] * bit_of(me_far, bit)
    me_set = 0
    for far in range(far_count):
        for side in range(side_count):
            if sets[far][side]:
                me_set = jnp.where((me_far == far) & (me_side == side), sets[far][side], me_set)
    earlier = 0
    for key, _, _ in chips_by_key:
        earlier = earlier + jnp.where(key < me_key, 1, 0)
    pair, relay = set_count, set_count + 1

    def at(far, side, core):
        near = side & ((1 << near_bits) - 1)
        return ((side >> near_bits) * 2 + core, (far << near_bits) + near)

    def tell(semaphore, device):
        pl.semaphore_signal(semaphore, inc=1, device_id=device, device_id_type=MESH)

    barrier = pltpu.get_barrier_semaphore()

    @pl.when(me_core == 0)
    def _():
        tell(barrier, partner)

    for load in loads:
        load.start()

    for key, far, side in reversed(chips_by_key):
        @pl.when(me_key < key)
        def _(far=far, side=side):
            tell(barrier, at(far, side, 0))

    swaps = [
        pltpu.make_async_remote_copy(
            src_ref=source, dst_ref=target, send_sem=swap_send.at[spot], recv_sem=swap_recv.at[spot],
            device_id=partner, device_id_type=MESH,
        )
        for spot, (source, target) in enumerate(
            [(signs_hbm, signs_ref.at[me_core]), (panel_hbm.at[other_rows, :], panel_ref.at[me_core])]
        )
    ]

    @pl.when(me_core == 1)
    def _():
        pl.semaphore_wait(barrier, 1)
        tell(ready_sem.at[pair], partner)

    @pl.when(me_core == 0)
    def _():
        pl.semaphore_wait(ready_sem.at[pair], 1)

    for swap in swaps:
        swap.start()

    def settle():
        @pl.when(earlier > 0)
        def _():
            pl.semaphore_wait(barrier, 2 * earlier)

        tell(ready_sem.at[relay], partner)
        for key, far, side in chips_by_key:
            @pl.when(me_key > key)
            def _(far=far, side=side):
                for core in range(2):
                    tell(ready_sem.at[me_set], at(far, side, core))

    @pl.when((me_core == 0) & (me_side == side_count - 1))
    def _():
        settle()

    core_bit = log2(local_rows) + inner_bits
    chip_at = [log2(local_rows) + bit for bit in range(inner_bits)]
    chip_at += [core_bit + 1 + bit for bit in range(chip_bits - inner_bits)]
    fold_bits = [core_bit] + [bit for bit in reversed(range(log2(DEPTH), log2(local_rows)))]

    loads[0].wait()

    def signs_of(tile, carry):
        first = jnp.right_shift(tile, inner_bits) * 2 * inner_count + jnp.bitwise_and(tile, inner_count - 1)
        kept = jnp.concatenate(
            [
                kept_ref[:, pl.ds(pl.multiple_of(block * LANES, LANES), LANES)]
                for block in (first, first + inner_count)
            ],
            axis=1,
        )
        width = 2 * LANES
        for spot, bit in enumerate(fold_bits):
            bits_ref[tile, spot:spot + 1, :] = sign_of_bit(kept, bit)
        plane = jnp.full((1, width), scale, jnp.float32)
        for bit, position in enumerate(chip_at):
            plane = plane * jnp.where(bit_of(me_chip, bit) == 1, sign_of_bit(kept, position), 1.0)
        bits_ref[tile, len(fold_bits):len(fold_bits) + 1, :] = plane
        position = lax.broadcasted_iota(jnp.int32, (PACK, width), 0)
        base = jnp.ones((PACK, width), jnp.float32)
        for bit in range(log2(PACK)):
            taken = jnp.bitwise_and(jnp.right_shift(position, bit), 1) == 1
            base = base * jnp.where(taken, sign_of_bit(kept, bit), 1.0)
        blocks = [base.astype(jnp.bfloat16)]
        for bit in range(log2(PACK), log2(DEPTH)):
            flip = jnp.broadcast_to(sign_of_bit(kept, bit), (PACK, width)).astype(jnp.bfloat16)
            blocks = blocks + [block * flip for block in blocks]
        for top, block in enumerate(blocks):
            mix_ref[tile, top * PACK:(top + 1) * PACK, :] = block
        return carry

    lax.fori_loop(0, chip_count, signs_of, 0)

    @pl.when((me_core == 0) & (me_side > 0) & (me_side < side_count - 1))
    def _():
        settle()


    def split(core):
        for mid in range(mids):
            lanes = slice(mid * DEPTH, (mid + 1) * DEPTH)
            block = panel_ref[core, :, lanes] * signs_ref[core, :, lanes].astype(jnp.float32)
            upper = block.astype(jnp.bfloat16)
            lower = (block - upper.astype(jnp.float32)).astype(jnp.bfloat16)
            upper_ref[core, mid * half:(mid + 1) * half, :] = upper
            lower_ref[core, mid * half:(mid + 1) * half, :] = lower

    for load in loads[1:]:
        load.wait()
    split(me_core)
    for swap in swaps:
        swap.wait_recv()
    split(1 - me_core)

    def parts_of(tiles):
        upper = upper_ref[...].reshape(rows, DEPTH)
        lower = lower_ref[...].reshape(rows, DEPTH)
        parts = []
        for tile in tiles:
            mix = mix_ref[tile]
            part = jnp.dot(upper, mix, preferred_element_type=jnp.float32)
            parts.append(part + jnp.dot(lower, mix, preferred_element_type=jnp.float32))
        for spot in range(len(fold_bits)):
            size = rows >> (spot + 1)
            parts = [
                part[:size] + part[size:] * bits_ref[tile, spot:spot + 1, :] for part, tile in zip(parts, tiles)
            ]
        plane = len(fold_bits)
        return [part * bits_ref[tile, plane:plane + 1, :] for part, tile in zip(parts, tiles)]

    mine = me_chip * 2 + me_core

    def own_at(slot):
        @pl.when(me_core == 0)
        def _():
            recv_ref[mine] = send_ref[slot]

        @pl.when(me_core == 1)
        def _():
            recv_ref[mine] = send_ref[slot + 1]

    def start(slot, chip, core):
        pltpu.make_async_remote_copy(
            src_ref=send_ref.at[slot + core],
            dst_ref=recv_ref.at[mine],
            send_sem=send_sem,
            recv_sem=recv_sem,
            device_id=(jnp.right_shift(chip, inner_bits) * 2 + core, jnp.bitwise_and(chip, inner_count - 1)),
            device_id_type=MESH,
        ).start()

    def start_both(slot, chip, maybe_own):
        cores = (0, 1) if slot == 0 else (1, 0)
        if not maybe_own:
            for core in cores:
                start(slot, chip, core)
            return
        own = chip == me_chip
        for core in cores:
            @pl.when(jnp.logical_not(own & (me_core == core)))
            def _(core=core):
                start(slot, chip, core)

        @pl.when(own)
        def _():
            own_at(slot)

    def keep(slot, part):
        send_ref[slot] = part[:, :LANES]
        send_ref[slot + 1] = part[:, LANES:]

    plans = routes(far_count, side_count)

    def by_row(values):
        picked = values[0]
        for row, value in enumerate(values[1:], 1):
            if value != values[0]:
                picked = jnp.where(me_far == row, value, picked)
        return picked

    def waited(chosen):
        total = 0
        for key, far, side in chips_by_key:
            if sets[far][side] == chosen:
                total = total + jnp.where(key > me_key, 1, 0)
        return total

    wanted = [waited(chosen) for chosen in range(set_count)]
    opened = [set() for _ in range(far_count)]
    place = 0
    for size in GROUPS if chip_count == sum(GROUPS) else [1] * chip_count:
        chips = []
        for spot in range(place, place + size):
            far = by_row([plan[spot][0] for plan in plans])
            swapped = by_row([plan[spot][1] % side_count for plan in plans])
            for row, plan in enumerate(plans):
                value = None
                if LEADS[row % len(LEADS)] and plan[spot][0] == 0:
                    start_spot = min(index for index, one in enumerate(plan) if one[0] == 0)
                    lead = plan[start_spot][1]
                    value = me_side if spot == start_spot else jnp.where(swapped == me_side, lead, swapped)
                elif plan[spot][1] >= side_count:
                    value = jnp.bitwise_xor(me_side, plan[spot][1] - side_count)
                if value is not None:
                    swapped = jnp.where(me_far == row, value, swapped)
            side = jnp.bitwise_xor(me_side, swapped)
            upper = jnp.right_shift(side, near_bits) * inner_count
            chips.append(upper + far * (1 << near_bits) + jnp.bitwise_and(side, (1 << near_bits) - 1))
        for spot, part in enumerate(parts_of(chips), place):
            keep(spot * 2, part)
        if place == 0:
            @pl.when((me_core == 0) & (me_side == 0))
            def _():
                settle()

            @pl.when(me_core == 1)
            def _():
                pl.semaphore_wait(ready_sem.at[relay], 1)

        for spot, chip in enumerate(chips, place):
            fresh = {}
            for row, plan in enumerate(plans):
                far, side = plan[spot]
                reached = [sets[far][side - side_count]] if side >= side_count else sets[far]
                for chosen in sorted(set(reached) - opened[row]):
                    opened[row].add(chosen)
                    fresh.setdefault(chosen, []).append(row)
            for chosen, opening in fresh.items():
                here = me_far == opening[0]
                for row in opening[1:]:
                    here = here | (me_far == row)

                @pl.when(here & (wanted[chosen] > 0))
                def _(chosen=chosen):
                    pl.semaphore_wait(ready_sem.at[chosen], wanted[chosen])

            own = any(
                plan[spot][0] == row and (plan[spot][1] % side_count == 0 or plan[spot][1] >= side_count or row == 0)
                for row, plan in enumerate(plans)
            )
            start_both(spot * 2, chip, own)
        place += size
    for swap in swaps:
        swap.wait_send()
    everything = pltpu.make_async_remote_copy(
        src_ref=send_ref.at[pl.ds(0, device_count - 1)],
        dst_ref=recv_ref.at[pl.ds(0, device_count - 1)],
        send_sem=send_sem,
        recv_sem=recv_sem,
        device_id=partner,
        device_id_type=MESH,
    )
    everything.wait_send()
    everything.wait_recv()
    for core in range(2):
        terms = [recv_ref[chip * 2 + core] for chip in range(chip_count)]
        while len(terms) > 1:
            terms = [one + other for one, other in zip(terms[::2], terms[1::2])]
        out_ref[core * half:(core + 1) * half, :] = terms[0]


def solution(mesh):
    outer_count, inner_count = mesh.shape["outer"], mesh.shape["inner"]
    device_count = outer_count * inner_count

    def local(matrix_panel, row_signs, kept_rows):
        columns, local_rows = matrix_panel.shape
        kept_count = kept_rows.shape[0]
        half = columns // 2
        powers = all(size & (size - 1) == 0 for size in (outer_count, inner_count, local_rows))
        fits = (
            powers
            and outer_count % 2 == 0
            and device_count >= 4
            and columns % (2 * PACK) == 0
            and kept_count == device_count * LANES
            and local_rows % (2 * DEPTH) == 0
        )
        if not fits:
            return scatter_form(matrix_panel, row_signs, kept_rows)
        mids = local_rows // DEPTH
        chips = device_count // 2
        arrived = pl.pallas_call(
            functools.partial(kernel, outer_count, inner_count, 1.0 / math.sqrt(local_rows * device_count)),
            out_shape=pltpu.VMEM((columns, LANES), jnp.float32),
            in_specs=[pl.BlockSpec(memory_space=pl.ANY)] * 3,
            out_specs=pl.BlockSpec(memory_space=pltpu.VMEM),
            scratch_shapes=[
                pltpu.VMEM((2, half, local_rows), jnp.float32),
                pltpu.VMEM((2, 1, local_rows), jnp.int32),
                pltpu.VMEM((1, kept_count), jnp.int32),
                pltpu.VMEM((2, mids * half, DEPTH), jnp.bfloat16),
                pltpu.VMEM((2, mids * half, DEPTH), jnp.bfloat16),
                pltpu.VMEM((chips, DEPTH, 2 * LANES), jnp.bfloat16),
                pltpu.VMEM((chips, 8, 2 * LANES), jnp.float32),
                pltpu.VMEM((device_count, half, LANES), jnp.float32),
                pltpu.VMEM((device_count, half, LANES), jnp.float32),
                pltpu.SemaphoreType.DMA((3,)),
                pltpu.SemaphoreType.DMA((2,)),
                pltpu.SemaphoreType.DMA((2,)),
                pltpu.SemaphoreType.DMA(()),
                pltpu.SemaphoreType.DMA(()),
                pltpu.SemaphoreType.REGULAR((max(inner_count // 2 + 2, 8),)),
            ],
            compiler_params=pltpu.CompilerParams(collective_id=0, has_side_effects=True),
        )(matrix_panel, row_signs.reshape(1, local_rows), kept_rows.reshape(1, kept_count))
        return arrived.T

    return jax.shard_map(
        local,
        mesh=mesh,
        in_specs=(P(None, ("outer", "inner")), P(("outer", "inner")), P()),
        out_specs=P(("outer", "inner"), None),
        check_vma=False,
    )
```
